512 devices in a mesh: row: 32 (over z_lo, x), col: 16 (over y, z_hi, core).
Axes of the slice: x: 4, y: 4, z: 16 (z_hi: 2, z_lo: 8; z = z_hi * 8 + z_lo), core: 2. Of those that a mesh axis runs over, the one named last changes fastest.
Arguments:
- left_factors: bfloat16 [32, 512, 2048], P(None, 'row', 'col'), may hold values from -0.890625 to 0.890625
- right_factors: bfloat16 [512, 131072], P('col', 'row'), may hold values from -0.890625 to 0.890625
- amplitudes: bfloat16 [512, 512, 256], P('row', 'col'), may hold values from -0.0234375 to 0.0234375
- eps_left: float32 [32], P('col'), may hold values from 0.2 to 1.5
- eps_right: float32 [64], replicated, may hold values from 0.2 to 1.5
- pair_energy: float32 [256], P('row'), may hold values from -2 to -0.5
Outputs:
- update: float32 [256, 32, 64], P('row', 'col')
The draws below stay inside these ranges and needn't reach their ends.
All inputs are finite; a program needn't handle non-finite values.
Results may differ from the reference program's by a relative error of at most 0.0029.
Values may be sent and summed in bfloat16 or wider, within the bound.
A program may use at most 128 MiB of HBM per device.

```python
import math
import jax
import jax.numpy as jnp
from jax import lax

V = 512
NAUX = 2048
PAIRS = 256
AW = 32
BW = 64


def strengthened(array, stream_key, source, target, shards_of, factor):
    owner, partner = [(jnp.arange(array.shape[dim]) // (array.shape[dim] // shards_of)).reshape([-1 if axis == dim else 1 for axis in range(array.ndim)]) for dim in (source, target)]
    chosen = jax.random.permutation(stream_key, shards_of)[partner]
    strong = (owner == chosen) | (owner == (partner + shards_of // 2) % shards_of)
    return jnp.where(strong, factor * array, array)


def levels(key, dims, shards, least, largest):
    def one(axis_at, parts):
        steps = jax.random.uniform(jax.random.fold_in(jax.random.fold_in(key, 6), axis_at), (parts,), jnp.float32, least / len(shards), largest / len(shards))
        return jnp.repeat(jnp.exp(steps), dims[axis_at] // parts).reshape((-1,) + (1,) * (len(dims) - axis_at - 1))

    level = one(*shards[0])
    for cut in shards[1:]:
        level = level * one(*cut)
    return level


def noise(stream_key, shape, spread, limit, cuts=(), kind=jnp.bfloat16):
    level = levels(stream_key, shape, cuts, -0.22, 0.18) if cuts else 1.0
    values = jax.random.normal(stream_key, shape, jnp.float32) * spread * level
    return jnp.minimum(jnp.maximum(values, -limit), limit).astype(kind)


def noise_with(stream_key, extent, spread, reach, shards, heavy, kind=jnp.bfloat16):
    result = spread * jax.random.normal(stream_key, extent, jnp.float32)
    if shards:
        result = result * levels(stream_key, extent, shards, -0.22, 0.18)
    return jnp.clip(strengthened(result, jax.random.fold_in(stream_key, 3), *heavy), -reach, reach).astype(kind)


def setup_inputs(seed: int = 0) -> dict:
    seeds = jax.random.split(jax.random.key(seed), 7)
    return {
        "left_factors": noise(seeds[0], (AW, V, NAUX), (NAUX ** -0.25), 0.890625, ((1, 32), (2, 16))),
        "right_factors": noise(seeds[1], (V, NAUX * BW), (NAUX ** -0.25), 0.890625, ((0, 16), (1, 32))),
        "amplitudes": noise_with(seeds[2], (V, V, PAIRS), (V * V) ** -0.5, 0.0234375, ((0, 32), (1, 16)), (0, 2, 32, 2.75)),
        "eps_left": jnp.clip(jnp.exp(math.log(1.5) - 2.014903 * jax.random.uniform(seeds[3], (AW,), jnp.float32) ** levels(seeds[3], (AW,), ((0, 16),), -0.2, 0.2)), 0.2, 1.5),
        "eps_right": jnp.clip(jnp.exp(jax.random.uniform(seeds[4], (BW,), jnp.float32, math.log(0.2), math.log(1.5))), 0.2, 1.5),
        "pair_energy": jnp.clip(-2.0 + 1.5 * jax.random.uniform(seeds[5], (PAIRS,), jnp.float32) ** levels(seeds[5], (PAIRS,), ((0, 32),), -0.2, 0.2), -2.0, -0.5),
    }


def reference(left_factors, right_factors, amplitudes, eps_left, eps_right, pair_energy):
    right_full = right_factors.astype(jnp.float32).reshape(V, NAUX, BW)
    amp_full = amplitudes.astype(jnp.float32)

    def one_row(left_row):
        integ = jnp.einsum("cq,dqb->cdb", left_row.astype(jnp.float32), right_full, precision=lax.Precision.HIGHEST)
        integ = lax.optimization_barrier(integ.astype(jnp.bfloat16))
        integ = integ.astype(jnp.float32)
        return jnp.einsum("cdb,cdp->pb", integ, amp_full, precision=lax.Precision.HIGHEST)

    ladder = lax.map(one_row, left_factors)
    ladder = jnp.transpose(ladder, (1, 0, 2))
    denom = eps_left[None, :, None] + eps_right[None, None, :] - pair_energy[:, None, None]
    return ladder / denom
```

```python
import functools

import jax
import jax.numpy as jnp
from jax import lax
from jax.experimental import pallas as pl
from jax.experimental.pallas import tpu as pltpu
from jax.sharding import PartitionSpec as P

MESH = pl.DeviceIdType.MESH


def fused(
    lt_in, r_in, t_in, out_ref,
    rbuf, lt, relay, tbuf, lm, ibuf, acc, rs1, a2, x2a, x2b, a3, y3a, y3b, a4, r4,
    own_sem, r_send, r_recv, t_send, t_recv, s1_send, s1_recv, h_send, h_recv, y_send, y_recv,
    k_send, k_recv, c_send, c_recv, xa_send, xa_recv, xb_send, xb_recv,
    ya_send, ya_recv, yb_send, yb_recv, z_send, z_recv,
):
    row = lax.axis_index("row")
    col = lax.axis_index("col")
    x, zl = row % 4, row // 4
    y, zh, core = col // 4, (col // 2) % 2, col % 2
    z = zh * 8 + zl

    def dev(x_, y_, z_, core_):
        return {"row": (z_ % 8) * 4 + x_, "col": y_ * 4 + (z_ // 8) * 2 + core_}

    def remote(src, dst, send, recv, to):
        return pltpu.make_async_remote_copy(
            src_ref=src, dst_ref=dst, send_sem=send, recv_sem=recv, device_id=to, device_id_type=MESH
        )

    xp, xm, xo = (x + 1) % 4, (x + 3) % 4, (x + 2) % 4
    yp, ym, yo = (y + 1) % 4, (y + 3) % 4, (y + 2) % 4

    barrier = pltpu.get_barrier_semaphore()
    count = 0
    for dx in range(4):
        for dc in range(2):
            if dx or dc:
                pl.semaphore_signal(barrier, inc=1, device_id=dev((x + dx) % 4, y, z, (core + dc) % 2), device_id_type=MESH)
                count += 1
    for yn in (yp, ym):
        pl.semaphore_signal(barrier, inc=1, device_id=dev(x, yn, z, core), device_id_type=MESH)
        count += 1
    for dz in range(1, 16):
        pl.semaphore_signal(barrier, inc=1, device_id=dev(x, y, (z + dz) % 16, core), device_id_type=MESH)
        count += 1
    pl.semaphore_wait(barrier, count)

    has_up, has_down = zl < 7, zl > 0
    near_up, near_down = dev(x, y, (z + 1) % 16, core), dev(x, y, (z + 15) % 16, core)

    own_r = pltpu.make_async_copy(r_in, rbuf.at[zl], own_sem.at[0])
    own_t = pltpu.make_async_copy(t_in, tbuf.at[x], own_sem.at[1])
    own_r.start()
    own_t.start()

    s1 = []
    for h in range(2):
        x_to, core_to = 2 * core + h, x % 2
        here = (x_to == x) & (core_to == core)
        src = lt_in.at[pl.ds(64 * h, 64)]
        dst = lt.at[x % 2, y, zh, x // 2]
        away = remote(src, dst, s1_send.at[h], s1_recv.at[x // 2], dev(x_to, y, z, core_to))
        local = pltpu.make_async_copy(src, dst, s1_recv.at[x // 2])
        pl.when(jnp.logical_not(here))(away.start)
        pl.when(here)(local.start)
        s1.append((here, away))

    t_a = [
        remote(t_in, tbuf.at[x], t_send.at[0], t_recv.at[0], dev(xp, y, z, core)),
        remote(t_in, tbuf.at[x], t_send.at[1], t_recv.at[1], dev(xm, y, z, core)),
    ]
    for copy in t_a:
        copy.start()

    def up_copy(s, h):
        origin = jnp.maximum(zl - s, 0)
        src = r_in.at[h] if s == 0 else rbuf.at[origin, h]
        return remote(src, rbuf.at[origin, h], r_send.at[0, s, h], r_recv.at[0, s, h], near_up)

    def down_copy(s, h):
        origin = jnp.minimum(zl + s, 7)
        src = r_in.at[h] if s == 0 else rbuf.at[origin, h]
        return remote(src, rbuf.at[origin, h], r_send.at[1, s, h], r_recv.at[1, s, h], near_down)

    def r_step(s):
        for h in range(4):
            for copy_of, from_there, onward in (
                (up_copy, zl >= s, has_up),
                (down_copy, zl + s <= 7, has_down),
            ):
                if s > 0:
                    pl.when(from_there)(copy_of(s - 1, h).wait_recv)
                pl.when(from_there & onward)(copy_of(s, h).start)

    r_step(0)

    for m in range(2):
        pltpu.make_async_copy(lt.at[0, 0, 0, 0], lt.at[0, 0, 0, 0], s1_recv.at[m]).wait()
    ahead = jnp.where(core == 0, (z + 4) % 16, (z + 12) % 16)
    behind = jnp.where(core == 0, (z + 12) % 16, (z + 4) % 16)
    hop1 = remote(lt.at[core, y, zh], relay, h_send.at[0], h_recv.at[0], dev(x, y, ahead, core))
    hop1.start()
    r_step(1)
    hop1.wait_recv()
    hop2 = remote(relay, lt.at[core, y, behind // 8], h_send.at[1], h_recv.at[1], dev(x, y, ahead, core))
    hop2.start()
    for copy in t_a:
        copy.wait_recv()
    t_b = [
        remote(tbuf.at[xm, pl.ds(0, 256)], tbuf.at[xm, pl.ds(0, 256)], t_send.at[2], t_recv.at[2], dev(xp, y, z, core)),
        remote(tbuf.at[xp, pl.ds(256, 256)], tbuf.at[xp, pl.ds(256, 256)], t_send.at[3], t_recv.at[3], dev(xm, y, z, core)),
    ]
    for copy in t_b:
        copy.start()
    r_step(2)
    hop2.wait_recv()
    sibling = dev(x, y, z, 1 - core)
    y_a = [
        remote(lt.at[core, y], lt.at[core, y], y_send.at[0], y_recv.at[0], dev(x, yp, z, core)),
        remote(lt.at[core, y], lt.at[core, y], y_send.at[1], y_recv.at[1], dev(x, ym, z, core)),
    ]
    for copy in y_a:
        copy.start()
    share = [remote(lt.at[core, y_], lt.at[core, y_], k_send.at[i], k_recv.at[i], sibling) for i, y_ in enumerate((y, ym, yp, yo))]
    share[0].start()
    r_step(3)
    for copy in y_a:
        copy.wait_recv()
    y_b = [
        remote(lt.at[core, ym, 0], lt.at[core, ym, 0], y_send.at[2], y_recv.at[2], dev(x, yp, z, core)),
        remote(lt.at[core, yp, 1], lt.at[core, yp, 1], y_send.at[3], y_recv.at[3], dev(x, ym, z, core)),
    ]
    for copy in y_b:
        copy.start()
    share[1].start()
    share[2].start()
    r_step(4)
    for copy in y_b:
        copy.wait_recv()
    share[3].start()
    r_step(5)
    r_step(6)
    for copy in share:
        copy.wait_recv()
    for h in range(4):
        pl.when(zl >= 7)(up_copy(6, h).wait_recv)
        pl.when(zl <= 0)(down_copy(6, h).wait_recv)
    for copy in t_b:
        copy.wait_recv()
    own_r.wait()
    own_t.wait()

    for xs in range(4):
        piece = lt[xs % 2, :, :, xs // 2].reshape(512, 512)
        lm[xs] = piece.T

    @pl.loop(0, 8)
    def _(n):
        right = rbuf[:, :, :, pl.ds(pl.multiple_of(n * 256, 256), 256)].reshape(512, 256)
        for xs in range(4):
            value = jnp.dot(lm[xs], right, preferred_element_type=jnp.float32)
            ibuf[n, xs] = value.astype(jnp.bfloat16).reshape(32, 16, 256)

    lane = lax.broadcasted_iota(jnp.int32, (256, 128), 1)

    def ladder(ap):
        total = None
        for xs in range(4):
            sides = []
            for ai in range(2):
                tiles = [ibuf[j // 2, xs, 2 * ap + ai, :, 128 * (j % 2) : 128 * (j % 2) + 128] for j in range(16)]
                sides.append(jnp.concatenate(tiles, axis=0))
            rhs = jnp.concatenate(sides, axis=1)
            part = jnp.dot(tbuf[xs], rhs, preferred_element_type=jnp.float32)
            total = part if total is None else total + part
        even, odd = total[:256], total[256:]
        first = even[:, :128] + pltpu.roll(odd[:, :128], 64, 1)
        second = odd[:, 128:] + pltpu.roll(even[:, 128:], 64, 1)
        return jnp.where(lane < 64, first, second)

    def core_copy(i):
        return remote(acc.at[i], rs1.at[i], c_send.at[i], c_recv.at[i], sibling)

    @pl.loop(0, 8)
    def _(i):
        acc[i] = ladder(2 * i + (1 - core))
        core_copy(i).start()

    @pl.loop(0, 8)
    def _(i):
        value = ladder(2 * i + core)
        core_copy(i).wait_recv()
        a2[:, i] = (value + rs1[i]).reshape(4, 64, 128)

    x_a = [
        remote(a2.at[xo, pl.ds(0, 4)], x2a.at[0], xa_send.at[0], xa_recv.at[0], dev(xp, y, z, core)),
        remote(a2.at[xo, pl.ds(4, 4)], x2a.at[1], xa_send.at[1], xa_recv.at[1], dev(xm, y, z, core)),
    ]
    for copy in x_a:
        copy.start()
    x_a[0].wait_recv()
    a2[xp, 0:4] += x2a[0]
    x_a[1].wait_recv()
    a2[xm, 4:8] += x2a[1]
    x_b = [
        remote(a2.at[xp], x2b.at[0], xb_send.at[0], xb_recv.at[0], dev(xp, y, z, core)),
        remote(a2.at[xm], x2b.at[1], xb_send.at[1], xb_recv.at[1], dev(xm, y, z, core)),
    ]
    for copy in x_b:
        copy.start()
    for copy in x_b:
        copy.wait_recv()
    a3[...] = (a2[x] + x2b[0] + x2b[1]).reshape(4, 2, 64, 128)

    y_c = [
        remote(a3.at[yo, 0], y3a.at[0], ya_send.at[0], ya_recv.at[0], dev(x, yp, z, core)),
        remote(a3.at[yo, 1], y3a.at[1], ya_send.at[1], ya_recv.at[1], dev(x, ym, z, core)),
    ]
    for copy in y_c:
        copy.start()
    y_c[0].wait_recv()
    a3[yp, 0] += y3a[0]
    y_c[1].wait_recv()
    a3[ym, 1] += y3a[1]
    y_d = [
        remote(a3.at[yp], y3b.at[0], yb_send.at[0], yb_recv.at[0], dev(x, yp, z, core)),
        remote(a3.at[ym], y3b.at[1], yb_send.at[1], yb_recv.at[1], dev(x, ym, z, core)),
    ]
    for copy in y_d:
        copy.start()
    for copy in y_d:
        copy.wait_recv()
    a4[...] = (a3[y] + y3b[0] + y3b[1]).reshape(16, 8, 128)

    def z_copy(dz):
        to = (z + dz) % 16
        return remote(a4.at[to], r4.at[dz - 1], z_send.at[dz - 1], z_recv.at[dz - 1], dev(x, y, to, core))

    for dz in range(1, 16):
        z_copy(dz).start()
    total = a4[z]
    for dz in range(1, 16):
        z_copy(dz).wait_recv()
        total = total + r4[dz - 1]
    out_ref[...] = total

    for here, away in s1:
        pl.when(jnp.logical_not(here))(away.wait_send)
    for s in range(7):
        for h in range(4):
            pl.when((zl >= s) & has_up)(up_copy(s, h).wait_send)
            pl.when((zl + s <= 7) & has_down)(down_copy(s, h).wait_send)
    for copy in [hop1, hop2] + t_a + t_b + y_a + y_b + share + x_a + x_b + y_c + y_d:
        copy.wait_send()
    for i in range(8):
        core_copy(i).wait_send()
    for dz in range(1, 16):
        z_copy(dz).wait_send()


def per_device(left_factors, right_factors, amplitudes, eps_left, eps_right, pair_energy):
    lt_in = left_factors.reshape(512, 128).T
    r_in = right_factors.reshape(32, 64, 64).transpose(1, 0, 2).reshape(4, 16, 2048)
    t_in = (
        amplitudes.reshape(16, 16, 2, 8, 4, 8).transpose(2, 4, 3, 5, 1, 0).reshape(512, 256)
    )
    bf16, f32 = jnp.bfloat16, jnp.float32
    dma = pltpu.SemaphoreType.DMA
    ladder = pl.pallas_call(
        fused,
        out_shape=jax.ShapeDtypeStruct((8, 128), f32),
        in_specs=[pl.BlockSpec(memory_space=pltpu.VMEM)] * 3,
        out_specs=pl.BlockSpec(memory_space=pltpu.VMEM),
        scratch_shapes=[
            pltpu.VMEM((8, 4, 16, 2048), bf16),
            pltpu.VMEM((2, 4, 2, 2, 64, 512), bf16),
            pltpu.VMEM((2, 64, 512), bf16),
            pltpu.VMEM((4, 512, 256), bf16),
            pltpu.VMEM((4, 512, 512), bf16),
            pltpu.VMEM((8, 4, 32, 16, 256), bf16),
            pltpu.VMEM((8, 256, 128), f32),
            pltpu.VMEM((8, 256, 128), f32),
            pltpu.VMEM((4, 8, 64, 128), f32),
            pltpu.VMEM((2, 4, 64, 128), f32),
            pltpu.VMEM((2, 8, 64, 128), f32),
            pltpu.VMEM((4, 2, 64, 128), f32),
            pltpu.VMEM((2, 64, 128), f32),
            pltpu.VMEM((2, 2, 64, 128), f32),
            pltpu.VMEM((16, 8, 128), f32),
            pltpu.VMEM((15, 8, 128), f32),
            dma((2,)),
            dma((2, 7, 4)), dma((2, 7, 4)),
            dma((4,)), dma((4,)),
            dma((2,)), dma((2,)),
            dma((2,)), dma((2,)),
            dma((4,)), dma((4,)),
            dma((4,)), dma((4,)),
            dma((8,)), dma((8,)),
            dma((2,)), dma((2,)),
            dma((2,)), dma((2,)),
            dma((2,)), dma((2,)),
            dma((2,)), dma((2,)),
            dma((15,)), dma((15,)),
        ],
        compiler_params=pltpu.CompilerParams(
            collective_id=0, has_side_effects=True, vmem_limit_bytes=60 * 1024 * 1024
        ),
    )(lt_in, r_in, t_in)
    ladder = ladder.reshape(8, 2, 64)
    denom = eps_left[None, :, None] + eps_right[None, None, :] - pair_energy[:, None, None]
    return ladder / denom


def solution(mesh):
    in_specs = (
        P(None, "row", "col"),
        P("col", "row"),
        P("row", "col", None),
        P("col"),
        P(),
        P("row"),
    )
    out_specs = P("row", "col", None)
    return jax.shard_map(
        per_device, mesh=mesh, in_specs=in_specs, out_specs=out_specs, check_vma=False
    )
```

```python
import jax
import jax.numpy as jnp
from jax import lax
from jax.experimental import pallas as pl
from jax.experimental.pallas import tpu as pltpu
from jax.sharding import PartitionSpec as P

MESH = pl.DeviceIdType.MESH
LAG = 3


def fused(
    left_ref, right_ref, amp_ref, out_ref,
    lraw, rraw, lt_own, rbuf, lt, relay, tbuf, tt, lm, ibuf, acc, rs1,
    sa, sb, xa1, xa2, yb1, yb2, sa3, sb3, ya3, ya4, xb3, xb4, a4, r4,
    own_sem, r_send, r_recv, t_send, t_recv, s1_send, s1_recv, h_send, h_recv, y_send, y_recv,
    k_send, k_recv, c_send, c_recv, sum_send, sum_recv, z_send, z_recv,
):
    f32, bf16 = jnp.float32, jnp.bfloat16
    row = lax.axis_index("row")
    col = lax.axis_index("col")
    x, zl = row % 4, row // 4
    y, zh, core = col // 4, (col // 2) % 2, col % 2
    z = zh * 8 + zl

    def dev(x_, y_, z_, core_):
        return {"row": (z_ % 8) * 4 + x_, "col": y_ * 4 + (z_ // 8) * 2 + core_}

    def remote(src, dst, send, recv, to):
        return pltpu.make_async_remote_copy(
            src_ref=src, dst_ref=dst, send_sem=send, recv_sem=recv, device_id=to, device_id_type=MESH
        )

    xp, xm, xo = (x + 1) % 4, (x + 3) % 4, (x + 2) % 4
    yp, ym, yo = (y + 1) % 4, (y + 3) % 4, (y + 2) % 4
    x_up, x_down = dev(xp, y, z, core), dev(xm, y, z, core)
    y_up, y_down = dev(x, yp, z, core), dev(x, ym, z, core)
    z_up, z_down = dev(x, y, (z + 1) % 16, core), dev(x, y, (z + 15) % 16, core)
    sibling = dev(x, y, z, 1 - core)

    barrier = pltpu.get_barrier_semaphore()
    partners = [dev(x, y, (z + dz) % 16, core) for dz in (8, 7, 9, 6, 10, 5, 11, 4, 12, 3, 13, 2, 14, 1, 15)]
    partners += [dev((x + dx) % 4, y, z, (core + dc) % 2) for dx in (2, 1, 3, 0) for dc in range(2) if dx or dc]
    partners += [y_up, y_down]
    for partner in partners:
        pl.semaphore_signal(barrier, inc=1, device_id=partner, device_id_type=MESH)

    own = [
        pltpu.make_async_copy(right_ref, rraw, own_sem.at[0]),
        pltpu.make_async_copy(left_ref, lraw, own_sem.at[1]),
        pltpu.make_async_copy(amp_ref, tbuf.at[x], own_sem.at[2]),
    ]
    for copy in own:
        copy.start()

    r_id = lax.broadcasted_iota(jnp.int32, (256, 256), 0)
    c_id = lax.broadcasted_iota(jnp.int32, (256, 256), 1)
    swap = ((r_id // 16 == c_id % 16) & (r_id % 16 == c_id // 16)).astype(f32).astype(bf16)
    own[0].wait()
    for g in range(4):
        rows = []
        for q2 in range(8):
            low = rraw[0:16, 1024 * g + 128 * q2 : 1024 * g + 128 * q2 + 128]
            high = rraw[16:32, 1024 * g + 128 * q2 : 1024 * g + 128 * q2 + 128]
            rows.append(jnp.concatenate([low[:, :64], high[:, :64]], axis=1))
            rows.append(jnp.concatenate([low[:, 64:], high[:, 64:]], axis=1))
        turned = jnp.dot(swap, jnp.concatenate(rows, axis=0), preferred_element_type=f32)
        turned = turned.astype(bf16).reshape(4, 4, 16, 128)
        rbuf[:, zl, :, 16 * g : 16 * g + 16, :] = turned
    own[1].wait()
    lt_own[...] = lraw[...].reshape(512, 128).T
    own[2].wait()
    pl.semaphore_wait(barrier, len(partners))

    s1 = []
    for h in range(2):
        x_to, core_to = 2 * core + h, x % 2
        here = (x_to == x) & (core_to == core)
        src = lt_own.at[pl.ds(64 * h, 64)]
        dst = lt.at[x % 2, y, zh, x // 2]
        away = remote(src, dst, s1_send.at[h], s1_recv.at[x // 2], dev(x_to, y, z, core_to))
        local = pltpu.make_async_copy(src, dst, s1_recv.at[x // 2])
        pl.when(jnp.logical_not(here))(away.start)
        pl.when(here)(local.start)
        s1.append((here, away))

    def right_copy(way, jc, s):
        origin = jnp.clip(zl - s, 0, 7) if way == 0 else jnp.clip(zl + s, 0, 7)
        block = rbuf.at[jc, origin]
        return remote(block, block, r_send.at[way, jc, s], r_recv.at[way, jc, s], z_up if way == 0 else z_down)

    def slot(tau):
        for jc in range(4):
            s = tau - LAG * jc
            for way in range(2):
                reach = zl if way == 0 else 7 - zl
                if not isinstance(s, int) or 1 <= s <= 7:
                    came = right_copy(way, jc, jnp.clip(s - 1, 0, 6))
                    pl.when((s >= 1) & (s <= reach))(came.wait_recv)
                if not isinstance(s, int) or 0 <= s <= 6:
                    goes = right_copy(way, jc, jnp.clip(s, 0, 6))
                    pl.when((s >= 0) & (s <= reach) & (s <= 6) & (reach < 7))(goes.start)

    t_a = [
        remote(tbuf.at[x], tbuf.at[x], t_send.at[0], t_recv.at[0], x_up),
        remote(tbuf.at[x], tbuf.at[x], t_send.at[1], t_recv.at[1], x_down),
    ]
    for copy in t_a:
        copy.start()
    slot(0)

    for m in range(2):
        pltpu.make_async_copy(lt.at[0, 0, 0, 0], lt.at[0, 0, 0, 0], s1_recv.at[m]).wait()
    ahead = jnp.where(core == 0, (z + 4) % 16, (z + 12) % 16)
    behind = jnp.where(core == 0, (z + 12) % 16, (z + 4) % 16)
    hop1 = remote(lt.at[core, y, zh], relay, h_send.at[0], h_recv.at[0], dev(x, y, ahead, core))
    hop1.start()
    acc[...] = jnp.zeros_like(acc)
    slot(1)
    slot(2)
    hop1.wait_recv()
    hop2 = remote(relay, lt.at[core, y, behind // 8], h_send.at[1], h_recv.at[1], dev(x, y, ahead, core))
    hop2.start()
    slot(3)
    for copy in t_a:
        copy.wait_recv()
    t_b = [
        remote(tbuf.at[xm, pl.ds(0, 8)], tbuf.at[xm, pl.ds(0, 8)], t_send.at[2], t_recv.at[2], x_up),
        remote(tbuf.at[xp, pl.ds(8, 8)], tbuf.at[xp, pl.ds(8, 8)], t_send.at[3], t_recv.at[3], x_down),
    ]
    for copy in t_b:
        copy.start()
    slot(4)
    slot(5)
    hop2.wait_recv()
    y_a = [
        remote(lt.at[core, y], lt.at[core, y], y_send.at[0], y_recv.at[0], y_up),
        remote(lt.at[core, y], lt.at[core, y], y_send.at[1], y_recv.at[1], y_down),
    ]
    for copy in y_a:
        copy.start()
    share = [remote(lt.at[core, y_], lt.at[core, y_], k_send.at[i], k_recv.at[i], sibling) for i, y_ in enumerate((y, ym, yp, yo))]
    share[0].start()
    slot(6)
    for copy in t_b:
        copy.wait_recv()

    r_id = lax.broadcasted_iota(jnp.int32, (512, 128), 0)
    c_id = lax.broadcasted_iota(jnp.int32, (512, 128), 1)
    for pair in range(2):
        for half in range(2):
            both = [tbuf[2 * pair + i, :, 16 * half : 16 * half + 16, :].reshape(256, 256) for i in range(2)]
            turned = jnp.concatenate(both, axis=0).T
            for jc in range(4):
                pick = (r_id // 256 == c_id // 64) & ((r_id // 16) % 16 == c_id % 16) & (r_id % 16 == 4 * jc + (c_id // 16) % 4)
                value = jnp.dot(turned, pick.astype(f32).astype(bf16), preferred_element_type=f32)
                tt[jc, 256 * half : 256 * half + 256, 128 * pair : 128 * pair + 128] = value.astype(bf16)
    slot(7)
    for copy in y_a:
        copy.wait_recv()
    y_b = [
        remote(lt.at[core, ym, 0], lt.at[core, ym, 0], y_send.at[2], y_recv.at[2], y_up),
        remote(lt.at[core, yp, 1], lt.at[core, yp, 1], y_send.at[3], y_recv.at[3], y_down),
    ]
    for copy in y_b:
        copy.start()
    share[1].start()
    share[2].start()
    slot(8)
    slot(9)
    for copy in y_b:
        copy.wait_recv()
    share[3].start()
    slot(10)

    for m in range(2):
        lm[2 * m + core] = lt[core, :, :, m].reshape(512, 512).T
    for copy in share:
        copy.wait_recv()
    for m in range(2):
        lm[2 * m + 1 - core] = lt[1 - core, :, :, m].reshape(512, 512).T

    def integrals(jc):
        @pl.loop(0, 2)
        def _(n):
            right = jnp.concatenate([rbuf[jc, :, 2 * n + i].reshape(512, 128) for i in range(2)], axis=1)
            for xs in range(4):
                value = jnp.dot(lm[xs], right, preferred_element_type=f32)
                ibuf[n, xs] = value.astype(bf16).reshape(32, 16, 256)

    lane = lax.broadcasted_iota(jnp.int32, (256, 128), 1)

    def ladder(jc, ap):
        sides = []
        for ai in range(2):
            tiles = [
                ibuf[j // 2, xs, 2 * ap + ai, :, 128 * (j % 2) : 128 * (j % 2) + 128]
                for xs in range(4) for j in range(4)
            ]
            sides.append(jnp.concatenate(tiles, axis=0))
        total = jnp.dot(tt[jc], jnp.concatenate(sides, axis=1), preferred_element_type=f32)
        even, odd = total[:256], total[256:]
        first = even[:, :128] + pltpu.roll(odd[:, :128], 64, 1)
        second = odd[:, 128:] + pltpu.roll(even[:, 128:], 64, 1)
        return jnp.where(lane < 64, first, second)

    def add_ladder(jc, low, high):
        @pl.loop(low, high)
        def _(ap):
            acc[ap] += ladder(jc, ap)

    @pl.loop(0, 3)
    def _(jc):
        integrals(jc)
        slot(11 + 3 * jc)
        add_ladder(jc, 0, 8)
        slot(12 + 3 * jc)
        add_ladder(jc, 8, 16)
        slot(13 + 3 * jc)

    integrals(3)

    def core_copy(i):
        return remote(acc.at[2 * i + 1 - core], rs1.at[i], c_send.at[i], c_recv.at[i], sibling)

    @pl.loop(0, 8)
    def _(i):
        acc[2 * i + 1 - core] += ladder(3, 2 * i + 1 - core)
        core_copy(i).start()

    @pl.loop(0, 8)
    def _(i):
        value = acc[2 * i + core] + ladder(3, 2 * i + core)
        core_copy(i).wait_recv()
        value = (value + rs1[i]).reshape(2, 4, 4, 8, 128)
        sa[:, i] = value[0].transpose(1, 0, 2, 3)
        sb[i // 2, i % 2] = value[1].transpose(1, 0, 2, 3)

    def sums(k, up_src, up_dst, down_src, down_dst, up, down):
        copies = [
            remote(up_src, up_dst, sum_send.at[k, 0], sum_recv.at[k, 0], up),
            remote(down_src, down_dst, sum_send.at[k, 1], sum_recv.at[k, 1], down),
        ]
        for copy in copies:
            copy.start()
        return copies

    a_1 = sums(0, sa.at[xo, pl.ds(0, 4)], xa1.at[0], sa.at[xo, pl.ds(4, 4)], xa1.at[1], x_up, x_down)
    b_1 = sums(1, sb.at[yo, 0], yb1.at[0], sb.at[yo, 1], yb1.at[1], y_up, y_down)
    a_1[0].wait_recv()
    sa[xp, 0:4] += xa1[0]
    a_1[1].wait_recv()
    sa[xm, 4:8] += xa1[1]
    a_2 = sums(2, sa.at[xp], xa2.at[0], sa.at[xm], xa2.at[1], x_up, x_down)
    b_1[0].wait_recv()
    sb[yp, 0] += yb1[0]
    b_1[1].wait_recv()
    sb[ym, 1] += yb1[1]
    b_2 = sums(3, sb.at[yp], yb2.at[0], sb.at[ym], yb2.at[1], y_up, y_down)
    for copy in a_2:
        copy.wait_recv()
    sa3[...] = (sa[x] + xa2[0] + xa2[1]).reshape(4, 2, 4, 8, 128)
    a_3 = sums(4, sa3.at[yo, 0], ya3.at[0], sa3.at[yo, 1], ya3.at[1], y_up, y_down)
    for copy in b_2:
        copy.wait_recv()
    sb3[...] = (sb[y] + yb2[0] + yb2[1]).transpose(1, 0, 2, 3, 4)
    b_3 = sums(5, sb3.at[xo, 0], xb3.at[0], sb3.at[xo, 1], xb3.at[1], x_up, x_down)
    for copy in a_3:
        copy.wait_recv()
    sa3[yp, 0] += ya3[0]
    sa3[ym, 1] += ya3[1]
    a_4 = sums(6, sa3.at[yp], ya4.at[0], sa3.at[ym], ya4.at[1], y_up, y_down)
    for copy in b_3:
        copy.wait_recv()
    sb3[xp, 0] += xb3[0]
    sb3[xm, 1] += xb3[1]
    b_4 = sums(7, sb3.at[xp], xb4.at[0], sb3.at[xm], xb4.at[1], x_up, x_down)
    for copy in a_4:
        copy.wait_recv()
    a4[:, 0:4] = sa3[y] + ya4[0] + ya4[1]
    for copy in b_4:
        copy.wait_recv()
    a4[:, 4:8] = sb3[x] + xb4[0] + xb4[1]

    def z_copy(dz):
        to = (z + dz) % 16
        return remote(a4.at[to // 8, to % 8], r4.at[dz - 1], z_send.at[dz - 1], z_recv.at[dz - 1], dev(x, y, to, core))

    order = (8, 7, 9, 6, 10, 5, 11, 4, 12, 3, 13, 2, 14, 1, 15)
    for dz in order:
        z_copy(dz).start()
    total = a4[zh, zl]
    for dz in order[::-1]:
        z_copy(dz).wait_recv()
        total = total + r4[dz - 1]
    out_ref[:, 0, :] = total[:, :64]
    out_ref[:, 1, :] = total[:, 64:]

    for here, away in s1:
        pl.when(jnp.logical_not(here))(away.wait_send)

    @pl.loop(0, 7)
    def _(s):
        for jc in range(4):
            pl.when((s <= zl) & (zl < 7))(right_copy(0, jc, s).wait_send)
            pl.when((s <= 7 - zl) & (zl > 0))(right_copy(1, jc, s).wait_send)

    for copy in [hop1, hop2] + t_a + t_b + y_a + y_b + share + a_1 + b_1 + a_2 + b_2 + a_3 + b_3 + a_4 + b_4:
        copy.wait_send()
    for i in range(8):
        core_copy(i).wait_send()
    for dz in order:
        z_copy(dz).wait_send()


def per_device(left_factors, right_factors, amplitudes, eps_left, eps_right, pair_energy):
    bf16, f32 = jnp.bfloat16, jnp.float32
    dma = pltpu.SemaphoreType.DMA
    ladder = pl.pallas_call(
        fused,
        out_shape=jax.ShapeDtypeStruct((8, 2, 64), f32),
        in_specs=[pl.BlockSpec(memory_space=pl.ANY)] * 3,
        out_specs=pl.BlockSpec(memory_space=pltpu.VMEM),
        scratch_shapes=[
            pltpu.VMEM((32, 16, 128), bf16),
            pltpu.VMEM((32, 4096), bf16),
            pltpu.VMEM((128, 512), bf16),
            pltpu.VMEM((4, 8, 4, 64, 128), bf16),
            pltpu.VMEM((2, 4, 2, 2, 64, 512), bf16),
            pltpu.VMEM((2, 64, 512), bf16),
            pltpu.VMEM((4, 16, 32, 256), bf16),
            pltpu.VMEM((4, 512, 256), bf16),
            pltpu.VMEM((4, 512, 512), bf16),
            pltpu.VMEM((2, 4, 32, 16, 256), bf16),
            pltpu.VMEM((16, 256, 128), f32),
            pltpu.VMEM((8, 256, 128), f32),
            pltpu.VMEM((4, 8, 4, 8, 128), f32),
            pltpu.VMEM((4, 2, 4, 4, 8, 128), f32),
            pltpu.VMEM((2, 4, 4, 8, 128), f32),
            pltpu.VMEM((2, 8, 4, 8, 128), f32),
            pltpu.VMEM((2, 4, 4, 8, 128), f32),
            pltpu.VMEM((2, 2, 4, 4, 8, 128), f32),
            pltpu.VMEM((4, 2, 4, 8, 128), f32),
            pltpu.VMEM((4, 2, 4, 8, 128), f32),
            pltpu.VMEM((2, 4, 8, 128), f32),
            pltpu.VMEM((2, 2, 4, 8, 128), f32),
            pltpu.VMEM((2, 4, 8, 128), f32),
            pltpu.VMEM((2, 2, 4, 8, 128), f32),
            pltpu.VMEM((2, 8, 8, 128), f32),
            pltpu.VMEM((15, 8, 128), f32),
            dma((3,)),
            dma((2, 4, 7)), dma((2, 4, 7)),
            dma((4,)), dma((4,)),
            dma((2,)), dma((2,)),
            dma((2,)), dma((2,)),
            dma((4,)), dma((4,)),
            dma((4,)), dma((4,)),
            dma((8,)), dma((8,)),
            dma((8, 2)), dma((8, 2)),
            dma((15,)), dma((15,)),
        ],
        compiler_params=pltpu.CompilerParams(
            collective_id=0, has_side_effects=True, vmem_limit_bytes=60 * 1024 * 1024
        ),
    )(left_factors, right_factors, amplitudes)
    denom = eps_left[None, :, None] + eps_right[None, None, :] - pair_energy[:, None, None]
    return ladder / denom


def solution(mesh):
    in_specs = (
        P(None, "row", "col"),
        P("col", "row"),
        P("row", "col", None),
        P("col"),
        P(),
        P("row"),
    )
    out_specs = P("row", "col", None)
    return jax.shard_map(
        per_device, mesh=mesh, in_specs=in_specs, out_specs=out_specs, check_vma=False
    )
```

```python
import jax
import jax.numpy as jnp
from jax import lax
from jax.experimental import pallas as pl
from jax.experimental.pallas import tpu as pltpu
from jax.sharding import PartitionSpec as P

MESH = pl.DeviceIdType.MESH
LAG = 1


def fused(
    left_ref, right_ref, amp_ref, out_ref,
    lraw, rraw, lt_own, rbuf, lt, relay, tbuf, tt, lm, ibuf, acc, rs1,
    sa, sb, xa1, xa2, yb1, yb2, sa3, sb3, ya3, ya4, xb3, xb4, a4, r4,
    own_sem, r_send, r_recv, t_send, t_recv, s1_send, s1_recv, h_send, h_recv, y_send, y_recv,
    k_send, k_recv, c_send, c_recv, sum_send, sum_recv, z_send, z_recv,
):
    f32, bf16 = jnp.float32, jnp.bfloat16
    row = lax.axis_index("row")
    col = lax.axis_index("col")
    x, zl = row % 4, row // 4
    y, zh, core = col // 4, (col // 2) % 2, col % 2
    z = zh * 8 + zl

    def dev(x_, y_, z_, core_):
        return {"row": (z_ % 8) * 4 + x_, "col": y_ * 4 + (z_ // 8) * 2 + core_}

    def remote(src, dst, send, recv, to):
        return pltpu.make_async_remote_copy(
            src_ref=src, dst_ref=dst, send_sem=send, recv_sem=recv, device_id=to, device_id_type=MESH
        )

    xp, xm, xo = (x + 1) % 4, (x + 3) % 4, (x + 2) % 4
    yp, ym, yo = (y + 1) % 4, (y + 3) % 4, (y + 2) % 4
    x_up, x_down = dev(xp, y, z, core), dev(xm, y, z, core)
    y_up, y_down = dev(x, yp, z, core), dev(x, ym, z, core)
    z_up, z_down = dev(x, y, (z + 1) % 16, core), dev(x, y, (z + 15) % 16, core)
    sibling = dev(x, y, z, 1 - core)

    barrier = pltpu.get_barrier_semaphore()
    partners = [dev(x, y, (z + dz) % 16, core) for dz in (8, 7, 9, 6, 10, 5, 11, 4, 12, 3, 13, 2, 14, 1, 15)]
    partners += [dev((x + dx) % 4, y, z, (core + dc) % 2) for dx in (2, 1, 3, 0) for dc in range(2) if dx or dc]
    partners += [y_up, y_down]
    for partner in partners:
        pl.semaphore_signal(barrier, inc=1, device_id=partner, device_id_type=MESH)

    own = [
        pltpu.make_async_copy(right_ref, rraw, own_sem.at[0]),
        pltpu.make_async_copy(left_ref, lraw, own_sem.at[1]),
        pltpu.make_async_copy(amp_ref, tbuf.at[x], own_sem.at[2]),
    ]
    for copy in own:
        copy.start()

    r_id = lax.broadcasted_iota(jnp.int32, (256, 256), 0)
    c_id = lax.broadcasted_iota(jnp.int32, (256, 256), 1)
    swap = ((r_id // 16 == c_id % 16) & (r_id % 16 == c_id // 16)).astype(f32).astype(bf16)
    own[0].wait()
    for g in range(4):
        rows = []
        for q2 in range(8):
            low = rraw[0:16, 1024 * g + 128 * q2 : 1024 * g + 128 * q2 + 128]
            high = rraw[16:32, 1024 * g + 128 * q2 : 1024 * g + 128 * q2 + 128]
            rows.append(jnp.concatenate([low[:, :64], high[:, :64]], axis=1))
            rows.append(jnp.concatenate([low[:, 64:], high[:, 64:]], axis=1))
        turned = jnp.dot(swap, jnp.concatenate(rows, axis=0), preferred_element_type=f32)
        turned = turned.astype(bf16).reshape(4, 4, 16, 128)
        rbuf[:, zl, :, 16 * g : 16 * g + 16, :] = turned
    own[1].wait()
    lt_own[...] = lraw[...].reshape(512, 128).T
    own[2].wait()
    pl.semaphore_wait(barrier, len(partners))

    s1 = []
    for h in range(2):
        x_to, core_to = 2 * core + h, x % 2
        here = (x_to == x) & (core_to == core)
        src = lt_own.at[pl.ds(64 * h, 64)]
        dst = lt.at[x % 2, y, zh, x // 2]
        away = remote(src, dst, s1_send.at[h], s1_recv.at[x // 2], dev(x_to, y, z, core_to))
        local = pltpu.make_async_copy(src, dst, s1_recv.at[x // 2])
        pl.when(jnp.logical_not(here))(away.start)
        pl.when(here)(local.start)
        s1.append((here, away))

    def right_copy(way, jc, s):
        origin = jnp.clip(zl - s, 0, 7) if way == 0 else jnp.clip(zl + s, 0, 7)
        block = rbuf.at[jc, origin]
        return remote(block, block, r_send.at[way, jc, s], r_recv.at[way, jc, s], z_up if way == 0 else z_down)

    def slot(tau):
        for jc in range(4):
            s = tau - LAG * jc
            for way in range(2):
                reach = zl if way == 0 else 7 - zl
                if not isinstance(s, int) or 1 <= s <= 7:
                    came = right_copy(way, jc, jnp.clip(s - 1, 0, 6))
                    pl.when((s >= 1) & (s <= reach))(came.wait_recv)
                if not isinstance(s, int) or 0 <= s <= 6:
                    goes = right_copy(way, jc, jnp.clip(s, 0, 6))
                    pl.when((s >= 0) & (s <= reach) & (s <= 6) & (reach < 7))(goes.start)

    t_a = [
        remote(tbuf.at[x], tbuf.at[x], t_send.at[0], t_recv.at[0], x_up),
        remote(tbuf.at[x], tbuf.at[x], t_send.at[1], t_recv.at[1], x_down),
    ]
    for copy in t_a:
        copy.start()

    slot(0)

    for m in range(2):
        pltpu.make_async_copy(lt.at[0, 0, 0, 0], lt.at[0, 0, 0, 0], s1_recv.at[m]).wait()
    ahead = jnp.where(core == 0, (z + 4) % 16, (z + 12) % 16)
    behind = jnp.where(core == 0, (z + 12) % 16, (z + 4) % 16)
    hop1 = remote(lt.at[core, y, zh], relay, h_send.at[0], h_recv.at[0], dev(x, y, ahead, core))
    hop1.start()
    acc[...] = jnp.zeros_like(acc)
    slot(1)
    slot(2)
    hop1.wait_recv()
    hop2 = remote(relay, lt.at[core, y, behind // 8], h_send.at[1], h_recv.at[1], dev(x, y, ahead, core))
    hop2.start()
    slot(3)
    for copy in t_a:
        copy.wait_recv()
    t_b = [
        remote(tbuf.at[xm, pl.ds(0, 8)], tbuf.at[xm, pl.ds(0, 8)], t_send.at[2], t_recv.at[2], x_up),
        remote(tbuf.at[xp, pl.ds(8, 8)], tbuf.at[xp, pl.ds(8, 8)], t_send.at[3], t_recv.at[3], x_down),
    ]
    for copy in t_b:
        copy.start()
    slot(4)
    hop2.wait_recv()
    y_a = [
        remote(lt.at[core, y], lt.at[core, y], y_send.at[0], y_recv.at[0], y_up),
        remote(lt.at[core, y], lt.at[core, y], y_send.at[1], y_recv.at[1], y_down),
    ]
    for copy in y_a:
        copy.start()
    share = [remote(lt.at[core, y_], lt.at[core, y_], k_send.at[i], k_recv.at[i], sibling) for i, y_ in enumerate((y, ym, yp, yo))]
    share[0].start()
    for copy in t_b:
        copy.wait_recv()

    r_id = lax.broadcasted_iota(jnp.int32, (512, 128), 0)
    c_id = lax.broadcasted_iota(jnp.int32, (512, 128), 1)
    for pair in range(2):
        for half in range(2):
            both = [tbuf[2 * pair + i, :, 16 * half : 16 * half + 16, :].reshape(256, 256) for i in range(2)]
            turned = jnp.concatenate(both, axis=0).T
            for jc in range(4):
                pick = (r_id // 256 == c_id // 64) & ((r_id // 16) % 16 == c_id % 16) & (r_id % 16 == 4 * jc + (c_id // 16) % 4)
                value = jnp.dot(turned, pick.astype(f32).astype(bf16), preferred_element_type=f32)
                tt[jc, :, 256 * half + 128 * pair : 256 * half + 128 * pair + 128] = value.astype(bf16)
    slot(5)
    for copy in y_a:
        copy.wait_recv()
    y_b = [
        remote(lt.at[core, ym, 0], lt.at[core, ym, 0], y_send.at[2], y_recv.at[2], y_up),
        remote(lt.at[core, yp, 1], lt.at[core, yp, 1], y_send.at[3], y_recv.at[3], y_down),
    ]
    for copy in y_b:
        copy.start()
    share[1].start()
    share[2].start()
    slot(6)
    for copy in y_b:
        copy.wait_recv()
    share[3].start()

    for m in range(2):
        lm[2 * m + core] = lt[core, :, :, m].reshape(512, 512).T
    slot(7)
    for copy in share:
        copy.wait_recv()
    for m in range(2):
        lm[2 * m + 1 - core] = lt[1 - core, :, :, m].reshape(512, 512).T

    def integrals(jc):
        @pl.loop(0, 2)
        def _(n):
            right = jnp.concatenate([rbuf[jc, :, 2 * n + i].reshape(512, 128) for i in range(2)], axis=1)
            for xs in range(4):
                value = jnp.dot(lm[xs], right, preferred_element_type=f32)
                ibuf[n, xs] = value.astype(bf16).reshape(32, 16, 256)

    def ladder(jc, first, second):
        low, high = [], []
        for ap in (first, second):
            sides = []
            for ai in range(2):
                tiles = [
                    ibuf[j // 2, xs, 2 * ap + ai, :, 128 * (j % 2) : 128 * (j % 2) + 128]
                    for xs in range(4) for j in range(4)
                ]
                sides.append(jnp.concatenate(tiles, axis=0))
            low += [side[:, :64] for side in sides]
            high += [side[:, 64:] for side in sides]
        both = jnp.concatenate([jnp.concatenate(low, axis=1), jnp.concatenate(high, axis=1)], axis=0)
        value = jnp.dot(tt[jc], both, preferred_element_type=f32)
        return value[:, :128], value[:, 128:]

    def add_ladder(jc, low, high):
        @pl.loop(low, high)
        def _(i):
            for k in range(2):
                one, two = ladder(jc, 4 * i + 2 * k, 4 * i + 2 * k + 1)
                acc[4 * i + 2 * k] += one
                acc[4 * i + 2 * k + 1] += two

    @pl.loop(0, 3)
    def _(jc):
        integrals(jc)
        slot(8 + jc)
        add_ladder(jc, 0, 4)

    integrals(3)

    def core_copy(i):
        return remote(acc.at[2 * i + 1 - core], rs1.at[i], c_send.at[i], c_recv.at[i], sibling)

    @pl.loop(0, 4)
    def _(k):
        first, second = 4 * k + 1 - core, 4 * k + 3 - core
        one, two = ladder(3, first, second)
        acc[first] += one
        core_copy(2 * k).start()
        acc[second] += two
        core_copy(2 * k + 1).start()

    @pl.loop(0, 4)
    def _(k):
        parts = ladder(3, 4 * k + core, 4 * k + 2 + core)
        for m in range(2):
            i = 2 * k + m
            value = acc[2 * i + core] + parts[m]
            core_copy(i).wait_recv()
            value = (value + rs1[i]).reshape(2, 4, 4, 8, 128)
            sa[:, i] = value[0].transpose(1, 0, 2, 3)
            sb[k, m] = value[1].transpose(1, 0, 2, 3)

    def sums(k, up_src, up_dst, down_src, down_dst, up, down):
        copies = [
            remote(up_src, up_dst, sum_send.at[k, 0], sum_recv.at[k, 0], up),
            remote(down_src, down_dst, sum_send.at[k, 1], sum_recv.at[k, 1], down),
        ]
        for copy in copies:
            copy.start()
        return copies

    a_1 = sums(0, sa.at[xo, pl.ds(0, 4)], xa1.at[0], sa.at[xo, pl.ds(4, 4)], xa1.at[1], x_up, x_down)
    b_1 = sums(1, sb.at[yo, 0], yb1.at[0], sb.at[yo, 1], yb1.at[1], y_up, y_down)
    a_1[0].wait_recv()
    sa[xp, 0:4] += xa1[0]
    a_1[1].wait_recv()
    sa[xm, 4:8] += xa1[1]
    a_2 = sums(2, sa.at[xp], xa2.at[0], sa.at[xm], xa2.at[1], x_up, x_down)
    b_1[0].wait_recv()
    sb[yp, 0] += yb1[0]
    b_1[1].wait_recv()
    sb[ym, 1] += yb1[1]
    b_2 = sums(3, sb.at[yp], yb2.at[0], sb.at[ym], yb2.at[1], y_up, y_down)
    for copy in a_2:
        copy.wait_recv()
    sa3[...] = (sa[x] + xa2[0] + xa2[1]).reshape(4, 2, 4, 8, 128)
    a_3 = sums(4, sa3.at[yo, 0], ya3.at[0], sa3.at[yo, 1], ya3.at[1], y_up, y_down)
    for copy in b_2:
        copy.wait_recv()
    sb3[...] = (sb[y] + yb2[0] + yb2[1]).transpose(1, 0, 2, 3, 4)
    b_3 = sums(5, sb3.at[xo, 0], xb3.at[0], sb3.at[xo, 1], xb3.at[1], x_up, x_down)
    for copy in a_3:
        copy.wait_recv()
    sa3[yp, 0] += ya3[0]
    sa3[ym, 1] += ya3[1]
    a_4 = sums(6, sa3.at[yp], ya4.at[0], sa3.at[ym], ya4.at[1], y_up, y_down)
    for copy in b_3:
        copy.wait_recv()
    sb3[xp, 0] += xb3[0]
    sb3[xm, 1] += xb3[1]
    b_4 = sums(7, sb3.at[xp], xb4.at[0], sb3.at[xm], xb4.at[1], x_up, x_down)
    for copy in a_4:
        copy.wait_recv()
    a4[:, 0:4] = sa3[y] + ya4[0] + ya4[1]
    for copy in b_4:
        copy.wait_recv()
    a4[:, 4:8] = sb3[x] + xb4[0] + xb4[1]

    def z_copy(dz):
        to = (z + dz) % 16
        return remote(a4.at[to // 8, to % 8], r4.at[dz - 1], z_send.at[dz - 1], z_recv.at[dz - 1], dev(x, y, to, core))

    order = (8, 7, 9, 6, 10, 5, 11, 4, 12, 3, 13, 2, 14, 1, 15)
    for dz in order:
        z_copy(dz).start()
    total = a4[zh, zl]
    for dz in order[::-1]:
        z_copy(dz).wait_recv()
        total = total + r4[dz - 1]
    out_ref[:, 0, :] = total[:, :64]
    out_ref[:, 1, :] = total[:, 64:]

    for here, away in s1:
        pl.when(jnp.logical_not(here))(away.wait_send)

    @pl.loop(0, 7)
    def _(s):
        for jc in range(4):
            pl.when((s <= zl) & (zl < 7))(right_copy(0, jc, s).wait_send)
            pl.when((s <= 7 - zl) & (zl > 0))(right_copy(1, jc, s).wait_send)

    for copy in [hop1, hop2] + t_a + t_b + y_a + y_b + share + a_1 + b_1 + a_2 + b_2 + a_3 + b_3 + a_4 + b_4:
        copy.wait_send()
    for i in range(8):
        core_copy(i).wait_send()
    for dz in order:
        z_copy(dz).wait_send()


def per_device(left_factors, right_factors, amplitudes, eps_left, eps_right, pair_energy):
    bf16, f32 = jnp.bfloat16, jnp.float32
    dma = pltpu.SemaphoreType.DMA
    ladder = pl.pallas_call(
        fused,
        out_shape=jax.ShapeDtypeStruct((8, 2, 64), f32),
        in_specs=[pl.BlockSpec(memory_space=pl.ANY)] * 3,
        out_specs=pl.BlockSpec(memory_space=pltpu.VMEM),
        scratch_shapes=[
            pltpu.VMEM((32, 16, 128), bf16),
            pltpu.VMEM((32, 4096), bf16),
            pltpu.VMEM((128, 512), bf16),
            pltpu.VMEM((4, 8, 4, 64, 128), bf16),
            pltpu.VMEM((2, 4, 2, 2, 64, 512), bf16),
            pltpu.VMEM((2, 64, 512), bf16),
            pltpu.VMEM((4, 16, 32, 256), bf16),
            pltpu.VMEM((4, 256, 512), bf16),
            pltpu.VMEM((4, 512, 512), bf16),
            pltpu.VMEM((2, 4, 32, 16, 256), bf16),
            pltpu.VMEM((16, 256, 128), f32),
            pltpu.VMEM((8, 256, 128), f32),
            pltpu.VMEM((4, 8, 4, 8, 128), f32),
            pltpu.VMEM((4, 2, 4, 4, 8, 128), f32),
            pltpu.VMEM((2, 4, 4, 8, 128), f32),
            pltpu.VMEM((2, 8, 4, 8, 128), f32),
            pltpu.VMEM((2, 4, 4, 8, 128), f32),
            pltpu.VMEM((2, 2, 4, 4, 8, 128), f32),
            pltpu.VMEM((4, 2, 4, 8, 128), f32),
            pltpu.VMEM((4, 2, 4, 8, 128), f32),
            pltpu.VMEM((2, 4, 8, 128), f32),
            pltpu.VMEM((2, 2, 4, 8, 128), f32),
            pltpu.VMEM((2, 4, 8, 128), f32),
            pltpu.VMEM((2, 2, 4, 8, 128), f32),
            pltpu.VMEM((2, 8, 8, 128), f32),
            pltpu.VMEM((15, 8, 128), f32),
            dma((3,)),
            dma((2, 4, 7)), dma((2, 4, 7)),
            dma((4,)), dma((4,)),
            dma((2,)), dma((2,)),
            dma((2,)), dma((2,)),
            dma((4,)), dma((4,)),
            dma((4,)), dma((4,)),
            dma((8,)), dma((8,)),
            dma((8, 2)), dma((8, 2)),
            dma((15,)), dma((15,)),
        ],
        compiler_params=pltpu.CompilerParams(
            collective_id=0, has_side_effects=True, vmem_limit_bytes=60 * 1024 * 1024
        ),
    )(left_factors, right_factors, amplitudes)
    denom = eps_left[None, :, None] + eps_right[None, None, :] - pair_energy[:, None, None]
    return ladder / denom


def solution(mesh):
    in_specs = (
        P(None, "row", "col"),
        P("col", "row"),
        P("row", "col", None),
        P("col"),
        P(),
        P("row"),
    )
    out_specs = P("row", "col", None)
    return jax.shard_map(
        per_device, mesh=mesh, in_specs=in_specs, out_specs=out_specs, check_vma=False
    )
```

```python
import jax
import jax.numpy as jnp
from jax import lax
from jax.experimental import pallas as pl
from jax.experimental.pallas import tpu as pltpu
from jax.sharding import PartitionSpec as P

MESH = pl.DeviceIdType.MESH
LAG = 1


def fused(
    left_ref, right_ref, amp_ref, out_ref,
    lraw, rraw, lt_own, rbuf, lt, relay, tbuf, tt, lm, ibuf, acc,
    sa, sb, xa1, xa2, yb1, yb2, sa3, sb3, ya3, ya4, xb3, xb4, a4, r4,
    own_sem, r_send, r_recv, t_send, t_recv, s1_send, s1_recv, h_send, h_recv, y_send, y_recv,
    k_send, k_recv, c_send, c_recv, x_send, x_recv, sum_send, sum_recv, z_send, z_recv,
):
    f32, bf16 = jnp.float32, jnp.bfloat16
    row = lax.axis_index("row")
    col = lax.axis_index("col")
    x, zl = row % 4, row // 4
    y, zh, core = col // 4, (col // 2) % 2, col % 2
    z = zh * 8 + zl

    def dev(x_, y_, z_, core_):
        return {"row": (z_ % 8) * 4 + x_, "col": y_ * 4 + (z_ // 8) * 2 + core_}

    def remote(src, dst, send, recv, to):
        return pltpu.make_async_remote_copy(
            src_ref=src, dst_ref=dst, send_sem=send, recv_sem=recv, device_id=to, device_id_type=MESH
        )

    xp, xm, xo = (x + 1) % 4, (x + 3) % 4, (x + 2) % 4
    yp, ym, yo = (y + 1) % 4, (y + 3) % 4, (y + 2) % 4
    x_up, x_down = dev(xp, y, z, core), dev(xm, y, z, core)
    y_up, y_down = dev(x, yp, z, core), dev(x, ym, z, core)
    z_up, z_down = dev(x, y, (z + 1) % 16, core), dev(x, y, (z + 15) % 16, core)
    sibling = dev(x, y, z, 1 - core)

    barrier = pltpu.get_barrier_semaphore()
    partners = [dev(x, y, (z + dz) % 16, core) for dz in (8, 7, 9, 6, 10, 5, 11, 4, 12, 3, 13, 2, 14, 1, 15)]
    partners += [dev((x + dx) % 4, y, z, (core + dc) % 2) for dx in (2, 1, 3, 0) for dc in range(2) if dx or dc]
    partners += [y_up, y_down]
    for partner in partners:
        pl.semaphore_signal(barrier, inc=1, device_id=partner, device_id_type=MESH)

    own = [
        pltpu.make_async_copy(right_ref, rraw, own_sem.at[0]),
        pltpu.make_async_copy(left_ref, lraw, own_sem.at[1]),
        pltpu.make_async_copy(amp_ref, tbuf.at[core, x], own_sem.at[2]),
    ]
    for copy in own:
        copy.start()

    r_id = lax.broadcasted_iota(jnp.int32, (256, 256), 0)
    c_id = lax.broadcasted_iota(jnp.int32, (256, 256), 1)
    swap = ((r_id // 16 == c_id % 16) & (r_id % 16 == c_id // 16)).astype(f32).astype(bf16)
    own[0].wait()
    for g in range(4):
        rows = []
        for q2 in range(8):
            low = rraw[0:16, 1024 * g + 128 * q2 : 1024 * g + 128 * q2 + 128]
            high = rraw[16:32, 1024 * g + 128 * q2 : 1024 * g + 128 * q2 + 128]
            rows.append(jnp.concatenate([low[:, :64], high[:, :64]], axis=1))
            rows.append(jnp.concatenate([low[:, 64:], high[:, 64:]], axis=1))
        turned = jnp.dot(swap, jnp.concatenate(rows, axis=0), preferred_element_type=f32)
        turned = turned.astype(bf16).reshape(4, 4, 16, 128)
        rbuf[core, :, zl, :, 16 * g : 16 * g + 16, :] = turned
    own[1].wait()
    for half in range(2):
        lt_own[half] = lraw[:, half].reshape(256, 128).T
    own[2].wait()
    pl.semaphore_wait(barrier, len(partners))

    s1 = []
    for h in range(2):
        for half in range(2):
            x_to = 2 * core + h
            here = (x_to == x) & (core == half)
            src = lt_own.at[half, pl.ds(64 * h, 64)]
            dst = lt.at[y, zh, x]
            away = remote(src, dst, s1_send.at[h, half], s1_recv.at[x], dev(x_to, y, z, half))
            local = pltpu.make_async_copy(src, dst, s1_recv.at[x])
            pl.when(jnp.logical_not(here))(away.start)
            pl.when(here)(local.start)
            s1.append((here, away))

    def right_copy(way, jc, s):
        origin = jnp.clip(zl - s, 0, 7) if way == 0 else jnp.clip(zl + s, 0, 7)
        block = rbuf.at[core, jc, origin]
        return remote(block, block, r_send.at[way, jc, s], r_recv.at[way, jc, s], z_up if way == 0 else z_down)

    def chip_copy(jc, origin):
        block = rbuf.at[core, jc, origin]
        return remote(block, block, c_send.at[jc, origin], c_recv.at[jc, origin], sibling)

    def slot(tau):
        for jc in range(4):
            s = tau - LAG * jc
            for way in range(2):
                reach = zl if way == 0 else 7 - zl
                if not isinstance(s, int) or 1 <= s <= 7:
                    came = right_copy(way, jc, jnp.clip(s - 1, 0, 6))
                    pl.when((s >= 1) & (s <= reach))(came.wait_recv)
                if not isinstance(s, int) or 0 <= s <= 6:
                    goes = right_copy(way, jc, jnp.clip(s, 0, 6))
                    pl.when((s >= 0) & (s <= reach) & (s <= 6) & (reach < 7))(goes.start)
                origin = jnp.clip(zl - s, 0, 7) if way == 0 else jnp.clip(zl + s, 0, 7)
                if not isinstance(s, int) or way <= s <= 7:
                    pl.when((s >= way) & (s <= reach))(chip_copy(jc, origin).start)

    t_a = [
        remote(tbuf.at[core, x], tbuf.at[core, x], t_send.at[0], t_recv.at[0], x_up),
        remote(tbuf.at[core, x], tbuf.at[core, x], t_send.at[1], t_recv.at[1], x_down),
    ]
    for copy in t_a:
        copy.start()
    share = [
        remote(tbuf.at[core, x_], tbuf.at[core, x_], k_send.at[i], k_recv.at[i], sibling)
        for i, x_ in enumerate((x, xm, xp, xo))
    ]
    share[0].start()
    slot(0)

    for m in range(4):
        pltpu.make_async_copy(lt.at[0, 0, 0], lt.at[0, 0, 0], s1_recv.at[m]).wait()
    ahead = jnp.where(core == 0, (z + 4) % 16, (z + 12) % 16)
    behind = jnp.where(core == 0, (z + 12) % 16, (z + 4) % 16)
    hop1 = remote(lt.at[y, zh], relay, h_send.at[0], h_recv.at[0], dev(x, y, ahead, core))
    hop1.start()
    acc[...] = jnp.zeros_like(acc)
    slot(1)
    slot(2)
    hop1.wait_recv()
    hop2 = remote(relay, lt.at[y, behind // 8], h_send.at[1], h_recv.at[1], dev(x, y, ahead, core))
    hop2.start()
    slot(3)
    for copy in t_a:
        copy.wait_recv()
    t_b = [
        remote(tbuf.at[core, xm, pl.ds(0, 8)], tbuf.at[core, xm, pl.ds(0, 8)], t_send.at[2], t_recv.at[2], x_up),
        remote(tbuf.at[core, xp, pl.ds(8, 8)], tbuf.at[core, xp, pl.ds(8, 8)], t_send.at[3], t_recv.at[3], x_down),
    ]
    for copy in t_b:
        copy.start()
    share[1].start()
    share[2].start()
    slot(4)
    hop2.wait_recv()
    y_a = [
        remote(lt.at[y], lt.at[y], y_send.at[0], y_recv.at[0], y_up),
        remote(lt.at[y], lt.at[y], y_send.at[1], y_recv.at[1], y_down),
    ]
    for copy in y_a:
        copy.start()
    for copy in t_b:
        copy.wait_recv()
    share[3].start()
    slot(5)
    for copy in y_a:
        copy.wait_recv()
    y_b = [
        remote(lt.at[ym, 0], lt.at[ym, 0], y_send.at[2], y_recv.at[2], y_up),
        remote(lt.at[yp, 1], lt.at[yp, 1], y_send.at[3], y_recv.at[3], y_down),
    ]
    for copy in y_b:
        copy.start()
    slot(6)
    for copy in share:
        copy.wait_recv()

    r_id = lax.broadcasted_iota(jnp.int32, (512, 128), 0)
    c_id = lax.broadcasted_iota(jnp.int32, (512, 128), 1)
    for side in range(2):
        for pair in range(2):
            for half in range(2):
                both = [tbuf[side, 2 * pair + i, :, 16 * half : 16 * half + 16, :].reshape(256, 256) for i in range(2)]
                turned = jnp.concatenate(both, axis=0).T
                for jc in range(4):
                    pick = (r_id // 256 == c_id // 64) & ((r_id // 16) % 16 == c_id % 16) & (r_id % 16 == 4 * jc + (c_id // 16) % 4)
                    value = jnp.dot(turned, pick.astype(f32).astype(bf16), preferred_element_type=f32)
                    at = 512 * side + 256 * half + 128 * pair
                    tt[jc, :, at : at + 128] = value.astype(bf16)

    for copy in y_b:
        copy.wait_recv()
    for xs in range(4):
        lm[xs] = lt[:, :, xs].reshape(512, 256).T
    slot(7)

    def integrals(jc):
        for origin in range(8):
            chip_copy(jc, origin).wait_recv()

        @pl.loop(0, 4)
        def _(n):
            right = jnp.concatenate([rbuf[n // 2, jc, :, 2 * (n % 2) + i].reshape(512, 128) for i in range(2)], axis=1)
            for xs in range(4):
                value = jnp.dot(lm[xs], right, preferred_element_type=f32)
                ibuf[n, xs] = value.astype(bf16).reshape(16, 16, 256)

    def ladder(jc, k):
        rows = []
        for side in range(2):
            columns = []
            for ai in range(4):
                tiles = [
                    ibuf[2 * side + j // 2, xs, 4 * k + ai, :, 128 * (j % 2) : 128 * (j % 2) + 128]
                    for xs in range(4) for j in range(4)
                ]
                columns.append(jnp.concatenate(tiles, axis=0))
            rows.append(jnp.concatenate([column[:, :64] for column in columns], axis=1))
            rows.append(jnp.concatenate([column[:, 64:] for column in columns], axis=1))
        value = jnp.dot(tt[jc], jnp.concatenate(rows, axis=0), preferred_element_type=f32)
        return value[:, :128], value[:, 128:]

    @pl.loop(0, 3)
    def _(jc):
        integrals(jc)
        slot(8 + jc)

        @pl.loop(0, 2)
        def _(i):
            for k in (2 * i, 2 * i + 1):
                one, two = ladder(jc, k)
                acc[2 * k] += one
                acc[2 * k + 1] += two

    integrals(3)

    def first_copy(way, k):
        return remote(sa.at[xo, k, way], xa1.at[way, k], x_send.at[way, k], x_recv.at[way, k], (x_up, x_down)[way])

    def last_ladder(k):
        parts = ladder(3, k)
        for m in range(2):
            value = (acc[2 * k + m] + parts[m]).reshape(2, 4, 4, 8, 128)
            sa[:, k, m] = value[0].transpose(1, 0, 2, 3)
            sb[k, m] = value[1].transpose(1, 0, 2, 3)
        for way in range(2):
            first_copy(way, k).start()

    def sums(k, up_src, up_dst, down_src, down_dst, up, down):
        copies = [
            remote(up_src, up_dst, sum_send.at[k, 0], sum_recv.at[k, 0], up),
            remote(down_src, down_dst, sum_send.at[k, 1], sum_recv.at[k, 1], down),
        ]
        for copy in copies:
            copy.start()
        return copies

    last_ladder(yo)
    b_1 = sums(1, sb.at[yo, 0], yb1.at[0], sb.at[yo, 1], yb1.at[1], y_up, y_down)

    @pl.loop(1, 4)
    def _(k):
        last_ladder((yo + k) % 4)

    for way, x_ in enumerate((xp, xm)):
        for k in range(4):
            first_copy(way, k).wait_recv()
        sa[x_, :, way] += xa1[way]
    a_2 = sums(2, sa.at[xp], xa2.at[0], sa.at[xm], xa2.at[1], x_up, x_down)
    b_1[0].wait_recv()
    sb[yp, 0] += yb1[0]
    b_1[1].wait_recv()
    sb[ym, 1] += yb1[1]
    b_2 = sums(3, sb.at[yp], yb2.at[0], sb.at[ym], yb2.at[1], y_up, y_down)
    for copy in a_2:
        copy.wait_recv()
    sa3[...] = sa[x] + xa2[0] + xa2[1]
    a_3 = sums(4, sa3.at[yo, 0], ya3.at[0], sa3.at[yo, 1], ya3.at[1], y_up, y_down)
    for copy in b_2:
        copy.wait_recv()
    sb3[...] = (sb[y] + yb2[0] + yb2[1]).transpose(1, 0, 2, 3, 4)
    b_3 = sums(5, sb3.at[xo, 0], xb3.at[0], sb3.at[xo, 1], xb3.at[1], x_up, x_down)
    for copy in a_3:
        copy.wait_recv()
    sa3[yp, 0] += ya3[0]
    sa3[ym, 1] += ya3[1]
    a_4 = sums(6, sa3.at[yp], ya4.at[0], sa3.at[ym], ya4.at[1], y_up, y_down)
    for copy in b_3:
        copy.wait_recv()
    sb3[xp, 0] += xb3[0]
    sb3[xm, 1] += xb3[1]
    b_4 = sums(7, sb3.at[xp], xb4.at[0], sb3.at[xm], xb4.at[1], x_up, x_down)
    for copy in a_4:
        copy.wait_recv()
    a4[:, 0:4] = sa3[y] + ya4[0] + ya4[1]
    for copy in b_4:
        copy.wait_recv()
    a4[:, 4:8] = sb3[x] + xb4[0] + xb4[1]

    def z_copy(dz):
        to = (z + dz) % 16
        return remote(a4.at[to // 8, to % 8], r4.at[dz - 1], z_send.at[dz - 1], z_recv.at[dz - 1], dev(x, y, to, core))

    order = (8, 7, 9, 6, 10, 5, 11, 4, 12, 3, 13, 2, 14, 1, 15)
    for dz in order:
        z_copy(dz).start()
    total = a4[zh, zl]
    for dz in order[::-1]:
        z_copy(dz).wait_recv()
        total = total + r4[dz - 1]
    out_ref[:, 0, :] = total[:, :64]
    out_ref[:, 1, :] = total[:, 64:]

    for here, away in s1:
        pl.when(jnp.logical_not(here))(away.wait_send)

    @pl.loop(0, 7)
    def _(s):
        for jc in range(4):
            pl.when((s <= zl) & (zl < 7))(right_copy(0, jc, s).wait_send)
            pl.when((s <= 7 - zl) & (zl > 0))(right_copy(1, jc, s).wait_send)

    for jc in range(4):
        for origin in range(8):
            chip_copy(jc, origin).wait_send()

    for copy in [hop1, hop2] + t_a + t_b + y_a + y_b + share + b_1 + a_2 + b_2 + a_3 + b_3 + a_4 + b_4:
        copy.wait_send()
    for way in range(2):
        for k in range(4):
            first_copy(way, k).wait_send()
    for dz in order:
        z_copy(dz).wait_send()


def per_device(left_factors, right_factors, amplitudes, eps_left, eps_right, pair_energy):
    bf16, f32 = jnp.bfloat16, jnp.float32
    dma = pltpu.SemaphoreType.DMA
    ladder = pl.pallas_call(
        fused,
        out_shape=jax.ShapeDtypeStruct((8, 2, 64), f32),
        in_specs=[pl.BlockSpec(memory_space=pl.ANY)] * 3,
        out_specs=pl.BlockSpec(memory_space=pltpu.VMEM),
        scratch_shapes=[
            pltpu.VMEM((8, 2, 2, 16, 128), bf16),
            pltpu.VMEM((32, 4096), bf16),
            pltpu.VMEM((2, 128, 256), bf16),
            pltpu.VMEM((2, 4, 8, 4, 64, 128), bf16),
            pltpu.VMEM((4, 2, 4, 64, 256), bf16),
            pltpu.VMEM((4, 64, 256), bf16),
            pltpu.VMEM((2, 4, 16, 32, 256), bf16),
            pltpu.VMEM((4, 256, 1024), bf16),
            pltpu.VMEM((4, 256, 512), bf16),
            pltpu.VMEM((4, 4, 16, 16, 256), bf16),
            pltpu.VMEM((8, 256, 128), f32),
            pltpu.VMEM((4, 4, 2, 4, 8, 128), f32),
            pltpu.VMEM((4, 2, 4, 4, 8, 128), f32),
            pltpu.VMEM((2, 4, 4, 8, 128), f32),
            pltpu.VMEM((2, 4, 2, 4, 8, 128), f32),
            pltpu.VMEM((2, 4, 4, 8, 128), f32),
            pltpu.VMEM((2, 2, 4, 4, 8, 128), f32),
            pltpu.VMEM((4, 2, 4, 8, 128), f32),
            pltpu.VMEM((4, 2, 4, 8, 128), f32),
            pltpu.VMEM((2, 4, 8, 128), f32),
            pltpu.VMEM((2, 2, 4, 8, 128), f32),
            pltpu.VMEM((2, 4, 8, 128), f32),
            pltpu.VMEM((2, 2, 4, 8, 128), f32),
            pltpu.VMEM((2, 8, 8, 128), f32),
            pltpu.VMEM((15, 8, 128), f32),
            dma((3,)),
            dma((2, 4, 7)), dma((2, 4, 7)),
            dma((4,)), dma((4,)),
            dma((2, 2)), dma((4,)),
            dma((2,)), dma((2,)),
            dma((4,)), dma((4,)),
            dma((4,)), dma((4,)),
            dma((4, 8)), dma((4, 8)),
            dma((2, 4)), dma((2, 4)),
            dma((8, 2)), dma((8, 2)),
            dma((15,)), dma((15,)),
        ],
        compiler_params=pltpu.CompilerParams(
            collective_id=0, has_side_effects=True, vmem_limit_bytes=60 * 1024 * 1024
        ),
    )(left_factors.reshape(8, 2, 2, 16, 128), right_factors, amplitudes)
    denom = eps_left[None, :, None] + eps_right[None, None, :] - pair_energy[:, None, None]
    return ladder / denom


def solution(mesh):
    in_specs = (
        P(None, "row", "col"),
        P("col", "row"),
        P("row", "col", None),
        P("col"),
        P(),
        P("row"),
    )
    out_specs = P("row", "col", None)
    return jax.shard_map(
        per_device, mesh=mesh, in_specs=in_specs, out_specs=out_specs, check_vma=False
    )
```

```python
import jax
import jax.numpy as jnp
from jax import lax
from jax.experimental import pallas as pl
from jax.experimental.pallas import tpu as pltpu
from jax.sharding import PartitionSpec as P

MESH = pl.DeviceIdType.MESH
LAG = 1


def fused(
    left_ref, right_ref, amp_ref, eps_l, eps_r, pair_e, out_ref,
    lraw, rraw, lt_own, rbuf, lt, relay, tbuf, tt, lm, ibuf, acc,
    sa, sb, xa1, xa2, yb1, yb2, sa3, sb3, ya3, ya4, xb3, xb4, a4, r4,
    own_sem, r_send, r_recv, t_send, t_recv, s1_send, s1_recv, h_send, h_recv, y_send, y_recv,
    k_send, k_recv, c_send, c_recv, x_send, x_recv, sum_send, sum_recv, z_send, z_recv,
    line_sem,
):
    f32, bf16 = jnp.float32, jnp.bfloat16
    row = lax.axis_index("row")
    col = lax.axis_index("col")
    x, zl = row % 4, row // 4
    y, zh, core = col // 4, (col // 2) % 2, col % 2
    z = zh * 8 + zl

    def dev(x_, y_, z_, core_):
        return {"row": (z_ % 8) * 4 + x_, "col": y_ * 4 + (z_ // 8) * 2 + core_}

    def remote(src, dst, send, recv, to):
        return pltpu.make_async_remote_copy(
            src_ref=src, dst_ref=dst, send_sem=send, recv_sem=recv, device_id=to, device_id_type=MESH
        )

    xp, xm, xo = (x + 1) % 4, (x + 3) % 4, (x + 2) % 4
    yp, ym, yo = (y + 1) % 4, (y + 3) % 4, (y + 2) % 4
    x_up, x_down = dev(xp, y, z, core), dev(xm, y, z, core)
    y_up, y_down = dev(x, yp, z, core), dev(x, ym, z, core)
    z_up, z_down = dev(x, y, (z + 1) % 16, core), dev(x, y, (z + 15) % 16, core)
    sibling = dev(x, y, z, 1 - core)

    barrier = pltpu.get_barrier_semaphore()
    partners = [dev((x + dx) % 4, y, z, (core + dc) % 2) for dx in (2, 1, 3, 0) for dc in range(2) if dx or dc]
    partners += [y_up, y_down, z_up, z_down]
    for partner in partners:
        pl.semaphore_signal(barrier, inc=1, device_id=partner, device_id_type=MESH)

    own = [
        pltpu.make_async_copy(right_ref, rraw, own_sem.at[0]),
        pltpu.make_async_copy(left_ref, lraw, own_sem.at[1]),
        pltpu.make_async_copy(amp_ref, tbuf.at[core, x], own_sem.at[2]),
    ]
    for copy in own:
        copy.start()

    r_id = lax.broadcasted_iota(jnp.int32, (256, 256), 0)
    c_id = lax.broadcasted_iota(jnp.int32, (256, 256), 1)
    swap = ((r_id // 16 == c_id % 16) & (r_id % 16 == c_id // 16)).astype(f32).astype(bf16)
    own[0].wait()
    for g in range(4):
        rows = []
        for q2 in range(8):
            low = rraw[0:16, 1024 * g + 128 * q2 : 1024 * g + 128 * q2 + 128]
            high = rraw[16:32, 1024 * g + 128 * q2 : 1024 * g + 128 * q2 + 128]
            rows.append(jnp.concatenate([low[:, :64], high[:, :64]], axis=1))
            rows.append(jnp.concatenate([low[:, 64:], high[:, 64:]], axis=1))
        turned = jnp.dot(swap, jnp.concatenate(rows, axis=0), preferred_element_type=f32)
        turned = turned.astype(bf16).reshape(4, 4, 16, 128)
        rbuf[core, :, zl, :, 16 * g : 16 * g + 16, :] = turned
    own[1].wait()
    for half in range(2):
        lt_own[half] = lraw[:, half].reshape(256, 128).T
    own[2].wait()
    pl.semaphore_wait(barrier, len(partners))

    def heard(step):
        for way in range(2):
            pl.semaphore_wait(line_sem.at[step, way], 1)

    def tell(step):
        for way, to in enumerate((z_up, z_down)):
            pl.semaphore_signal(line_sem.at[step, way], inc=1, device_id=to, device_id_type=MESH)

    tell(0)

    s1 = []
    for h in range(2):
        for half in range(2):
            x_to = 2 * core + h
            here = (x_to == x) & (core == half)
            src = lt_own.at[half, pl.ds(64 * h, 64)]
            dst = lt.at[y, zh, x]
            away = remote(src, dst, s1_send.at[h, half], s1_recv.at[x], dev(x_to, y, z, half))
            local = pltpu.make_async_copy(src, dst, s1_recv.at[x])
            pl.when(jnp.logical_not(here))(away.start)
            pl.when(here)(local.start)
            s1.append((here, away))

    def right_copy(way, jc, s):
        origin = jnp.clip(zl - s, 0, 7) if way == 0 else jnp.clip(zl + s, 0, 7)
        block = rbuf.at[core, jc, origin]
        return remote(block, block, r_send.at[way, jc, s], r_recv.at[way, jc, s], z_up if way == 0 else z_down)

    def chip_copy(jc, origin):
        block = rbuf.at[core, jc, origin]
        return remote(block, block, c_send.at[jc, origin], c_recv.at[jc, origin], sibling)

    def slot(tau):
        for jc in range(4):
            s = tau - LAG * jc
            for way in range(2):
                reach = zl if way == 0 else 7 - zl
                if not isinstance(s, int) or 1 <= s <= 7:
                    came = right_copy(way, jc, jnp.clip(s - 1, 0, 6))
                    pl.when((s >= 1) & (s <= reach))(came.wait_recv)
                if not isinstance(s, int) or 0 <= s <= 6:
                    goes = right_copy(way, jc, jnp.clip(s, 0, 6))
                    pl.when((s >= 0) & (s <= reach) & (s <= 6) & (reach < 7))(goes.start)
                origin = jnp.clip(zl - s, 0, 7) if way == 0 else jnp.clip(zl + s, 0, 7)
                if not isinstance(s, int) or way <= s <= 7:
                    pl.when((s >= way) & (s <= reach))(chip_copy(jc, origin).start)

    t_a = [
        remote(tbuf.at[core, x], tbuf.at[core, x], t_send.at[0], t_recv.at[0], x_up),
        remote(tbuf.at[core, x], tbuf.at[core, x], t_send.at[1], t_recv.at[1], x_down),
    ]
    for copy in t_a:
        copy.start()
    share = [
        remote(tbuf.at[core, x_], tbuf.at[core, x_], k_send.at[i], k_recv.at[i], sibling)
        for i, x_ in enumerate((x, xm, xp, xo))
    ]
    share[0].start()
    slot(0)
    heard(0)
    tell(1)

    for m in range(4):
        pltpu.make_async_copy(lt.at[0, 0, 0], lt.at[0, 0, 0], s1_recv.at[m]).wait()
    heard(1)
    tell(2)
    heard(2)
    tell(3)
    ahead = jnp.where(core == 0, (z + 4) % 16, (z + 12) % 16)
    behind = jnp.where(core == 0, (z + 12) % 16, (z + 4) % 16)
    hop1 = remote(lt.at[y, zh], relay, h_send.at[0], h_recv.at[0], dev(x, y, ahead, core))
    hop1.start()
    acc[...] = jnp.zeros_like(acc)
    slot(1)
    heard(3)
    tell(4)
    slot(2)
    heard(4)
    tell(5)
    hop1.wait_recv()
    hop2 = remote(relay, lt.at[y, behind // 8], h_send.at[1], h_recv.at[1], dev(x, y, ahead, core))
    hop2.start()
    heard(5)
    tell(6)
    slot(3)
    heard(6)
    for copy in t_a:
        copy.wait_recv()
    t_b = [
        remote(tbuf.at[core, xm, pl.ds(0, 8)], tbuf.at[core, xm, pl.ds(0, 8)], t_send.at[2], t_recv.at[2], x_up),
        remote(tbuf.at[core, xp, pl.ds(8, 8)], tbuf.at[core, xp, pl.ds(8, 8)], t_send.at[3], t_recv.at[3], x_down),
    ]
    for copy in t_b:
        copy.start()
    share[1].start()
    share[2].start()
    slot(4)
    hop2.wait_recv()
    y_a = [
        remote(lt.at[y], lt.at[y], y_send.at[0], y_recv.at[0], y_up),
        remote(lt.at[y], lt.at[y], y_send.at[1], y_recv.at[1], y_down),
    ]
    for copy in y_a:
        copy.start()
    for copy in t_b:
        copy.wait_recv()
    share[3].start()
    slot(5)
    for copy in y_a:
        copy.wait_recv()
    y_b = [
        remote(lt.at[ym, 0], lt.at[ym, 0], y_send.at[2], y_recv.at[2], y_up),
        remote(lt.at[yp, 1], lt.at[yp, 1], y_send.at[3], y_recv.at[3], y_down),
    ]
    for copy in y_b:
        copy.start()
    slot(6)
    for copy in share:
        copy.wait_recv()

    r_id = lax.broadcasted_iota(jnp.int32, (512, 128), 0)
    c_id = lax.broadcasted_iota(jnp.int32, (512, 128), 1)
    for side in range(2):
        for pair in range(2):
            for half in range(2):
                both = [tbuf[side, 2 * pair + i, :, 16 * half : 16 * half + 16, :].reshape(256, 256) for i in range(2)]
                turned = jnp.concatenate(both, axis=0).T
                for jc in range(4):
                    pick = (r_id // 256 == c_id // 64) & ((r_id // 16) % 16 == c_id % 16) & (r_id % 16 == 4 * jc + (c_id // 16) % 4)
                    value = jnp.dot(turned, pick.astype(f32).astype(bf16), preferred_element_type=f32)
                    at = 512 * side + 256 * half + 128 * pair
                    tt[jc, :, at : at + 128] = value.astype(bf16)

    for copy in y_b:
        copy.wait_recv()
    for xs in range(4):
        lm[xs] = lt[:, :, xs].reshape(512, 256).T
    slot(7)

    def integrals(jc):
        for origin in range(8):
            chip_copy(jc, origin).wait_recv()

        @pl.loop(0, 4)
        def _(n):
            right = jnp.concatenate([rbuf[n // 2, jc, :, 2 * (n % 2) + i].reshape(512, 128) for i in range(2)], axis=1)
            for xs in range(4):
                value = jnp.dot(lm[xs], right, preferred_element_type=f32)
                ibuf[n, xs] = value.astype(bf16).reshape(16, 16, 256)

    def ladder(jc, k):
        rows = []
        for side in range(2):
            columns = []
            for ai in range(4):
                tiles = [
                    ibuf[2 * side + j // 2, xs, 4 * k + ai, :, 128 * (j % 2) : 128 * (j % 2) + 128]
                    for xs in range(4) for j in range(4)
                ]
                columns.append(jnp.concatenate(tiles, axis=0))
            rows.append(jnp.concatenate([column[:, :64] for column in columns], axis=1))
            rows.append(jnp.concatenate([column[:, 64:] for column in columns], axis=1))
        value = jnp.dot(tt[jc], jnp.concatenate(rows, axis=0), preferred_element_type=f32)
        return value[:, :128], value[:, 128:]

    @pl.loop(0, 3)
    def _(jc):
        integrals(jc)
        slot(8 + jc)

        @pl.loop(0, 2)
        def _(i):
            for k in (2 * i, 2 * i + 1):
                one, two = ladder(jc, k)
                acc[2 * k] += one
                acc[2 * k + 1] += two

    integrals(3)

    def first_copy(way, k):
        return remote(sa.at[xo, k, way], xa1.at[way, k], x_send.at[way, k], x_recv.at[way, k], (x_up, x_down)[way])

    def last_ladder(k):
        parts = ladder(3, k)
        for m in range(2):
            value = (acc[2 * k + m] + parts[m]).reshape(2, 4, 4, 8, 128)
            sa[:, k, m] = value[0].transpose(1, 0, 2, 3)
            sb[k, m] = value[1].transpose(1, 0, 2, 3)
        for way in range(2):
            first_copy(way, k).start()

    def sums(k, up_src, up_dst, down_src, down_dst, up, down):
        copies = [
            remote(up_src, up_dst, sum_send.at[k, 0], sum_recv.at[k, 0], up),
            remote(down_src, down_dst, sum_send.at[k, 1], sum_recv.at[k, 1], down),
        ]
        for copy in copies:
            copy.start()
        return copies

    last_ladder(yo)
    b_1 = sums(1, sb.at[yo, 0], yb1.at[0], sb.at[yo, 1], yb1.at[1], y_up, y_down)

    @pl.loop(1, 4)
    def _(k):
        last_ladder((yo + k) % 4)

    for way, x_ in enumerate((xp, xm)):
        for k in range(4):
            first_copy(way, k).wait_recv()
        sa[x_, :, way] += xa1[way]
    a_2 = sums(2, sa.at[xp], xa2.at[0], sa.at[xm], xa2.at[1], x_up, x_down)
    b_1[0].wait_recv()
    sb[yp, 0] += yb1[0]
    b_1[1].wait_recv()
    sb[ym, 1] += yb1[1]
    b_2 = sums(3, sb.at[yp], yb2.at[0], sb.at[ym], yb2.at[1], y_up, y_down)
    for copy in a_2:
        copy.wait_recv()
    sa3[...] = sa[x] + xa2[0] + xa2[1]
    a_3 = sums(4, sa3.at[yo, 0], ya3.at[0], sa3.at[yo, 1], ya3.at[1], y_up, y_down)
    for copy in b_2:
        copy.wait_recv()
    sb3[...] = (sb[y] + yb2[0] + yb2[1]).transpose(1, 0, 2, 3, 4)
    b_3 = sums(5, sb3.at[xo, 0], xb3.at[0], sb3.at[xo, 1], xb3.at[1], x_up, x_down)
    for copy in a_3:
        copy.wait_recv()
    sa3[yp, 0] += ya3[0]
    sa3[ym, 1] += ya3[1]
    a_4 = sums(6, sa3.at[yp], ya4.at[0], sa3.at[ym], ya4.at[1], y_up, y_down)
    for copy in b_3:
        copy.wait_recv()
    sb3[xp, 0] += xb3[0]
    sb3[xm, 1] += xb3[1]
    b_4 = sums(7, sb3.at[xp], xb4.at[0], sb3.at[xm], xb4.at[1], x_up, x_down)
    for copy in a_4:
        copy.wait_recv()
    a4[:, 0:4] = sa3[y] + ya4[0] + ya4[1]
    for copy in b_4:
        copy.wait_recv()
    a4[:, 4:8] = sb3[x] + xb4[0] + xb4[1]

    def z_copy(dz):
        to = (z + dz) % 16
        return remote(a4.at[to // 8, to % 8], r4.at[dz - 1], z_send.at[dz - 1], z_recv.at[dz - 1], dev(x, y, to, core))

    order = (8, 7, 9, 6, 10, 5, 11, 4, 12, 3, 13, 2, 14, 1, 15)
    for dz in order:
        z_copy(dz).start()
    total = a4[zh, zl]
    for dz in order[::-1]:
        z_copy(dz).wait_recv()
        total = total + r4[dz - 1]
    pair = lax.broadcasted_iota(jnp.int32, (8, 64), 0)
    energy = jnp.full((8, 64), pair_e[0], f32)
    for i in range(1, 8):
        energy = jnp.where(pair == i, pair_e[i], energy)
    for i in range(2):
        out_ref[:, i, :] = total[:, 64 * i : 64 * i + 64] / (eps_l[i] + eps_r[...] - energy)

    for here, away in s1:
        pl.when(jnp.logical_not(here))(away.wait_send)

    @pl.loop(0, 7)
    def _(s):
        for jc in range(4):
            pl.when((s <= zl) & (zl < 7))(right_copy(0, jc, s).wait_send)
            pl.when((s <= 7 - zl) & (zl > 0))(right_copy(1, jc, s).wait_send)

    for jc in range(4):
        for origin in range(8):
            chip_copy(jc, origin).wait_send()

    for copy in [hop1, hop2] + t_a + t_b + y_a + y_b + share + b_1 + a_2 + b_2 + a_3 + b_3 + a_4 + b_4:
        copy.wait_send()
    for way in range(2):
        for k in range(4):
            first_copy(way, k).wait_send()
    for dz in order:
        z_copy(dz).wait_send()


def per_device(left_factors, right_factors, amplitudes, eps_left, eps_right, pair_energy):
    bf16, f32 = jnp.bfloat16, jnp.float32
    dma = pltpu.SemaphoreType.DMA
    return pl.pallas_call(
        fused,
        out_shape=jax.ShapeDtypeStruct((8, 2, 64), f32),
        in_specs=[pl.BlockSpec(memory_space=pl.ANY)] * 3
        + [pl.BlockSpec(memory_space=space) for space in (pltpu.SMEM, pltpu.VMEM, pltpu.SMEM)],
        out_specs=pl.BlockSpec(memory_space=pltpu.VMEM),
        scratch_shapes=[
            pltpu.VMEM((8, 2, 2, 16, 128), bf16),
            pltpu.VMEM((32, 4096), bf16),
            pltpu.VMEM((2, 128, 256), bf16),
            pltpu.VMEM((2, 4, 8, 4, 64, 128), bf16),
            pltpu.VMEM((4, 2, 4, 64, 256), bf16),
            pltpu.VMEM((4, 64, 256), bf16),
            pltpu.VMEM((2, 4, 16, 32, 256), bf16),
            pltpu.VMEM((4, 256, 1024), bf16),
            pltpu.VMEM((4, 256, 512), bf16),
            pltpu.VMEM((4, 4, 16, 16, 256), bf16),
            pltpu.VMEM((8, 256, 128), f32),
            pltpu.VMEM((4, 4, 2, 4, 8, 128), f32),
            pltpu.VMEM((4, 2, 4, 4, 8, 128), f32),
            pltpu.VMEM((2, 4, 4, 8, 128), f32),
            pltpu.VMEM((2, 4, 2, 4, 8, 128), f32),
            pltpu.VMEM((2, 4, 4, 8, 128), f32),
            pltpu.VMEM((2, 2, 4, 4, 8, 128), f32),
            pltpu.VMEM((4, 2, 4, 8, 128), f32),
            pltpu.VMEM((4, 2, 4, 8, 128), f32),
            pltpu.VMEM((2, 4, 8, 128), f32),
            pltpu.VMEM((2, 2, 4, 8, 128), f32),
            pltpu.VMEM((2, 4, 8, 128), f32),
            pltpu.VMEM((2, 2, 4, 8, 128), f32),
            pltpu.VMEM((2, 8, 8, 128), f32),
            pltpu.VMEM((15, 8, 128), f32),
            dma((3,)),
            dma((2, 4, 7)), dma((2, 4, 7)),
            dma((4,)), dma((4,)),
            dma((2, 2)), dma((4,)),
            dma((2,)), dma((2,)),
            dma((4,)), dma((4,)),
            dma((4,)), dma((4,)),
            dma((4, 8)), dma((4, 8)),
            dma((2, 4)), dma((2, 4)),
            dma((8, 2)), dma((8, 2)),
            dma((15,)), dma((15,)),
            pltpu.SemaphoreType.REGULAR((7, 2)),
        ],
        compiler_params=pltpu.CompilerParams(
            collective_id=0, has_side_effects=True, vmem_limit_bytes=60 * 1024 * 1024
        ),
    )(
        left_factors.reshape(8, 2, 2, 16, 128), right_factors, amplitudes,
        eps_left, eps_right.reshape(1, 64), pair_energy,
    )


def solution(mesh):
    in_specs = (
        P(None, "row", "col"),
        P("col", "row"),
        P("row", "col", None),
        P("col"),
        P(),
        P("row"),
    )
    out_specs = P("row", "col", None)
    return jax.shard_map(
        per_device, mesh=mesh, in_specs=in_specs, out_specs=out_specs, check_vma=False
    )
```

```python
import jax
import jax.numpy as jnp
from jax import lax
from jax.experimental import pallas as pl
from jax.experimental.pallas import tpu as pltpu
from jax.sharding import PartitionSpec as P

MESH = pl.DeviceIdType.MESH
LAG = 1


def fused(
    left_ref, right_ref, amp_ref, eps_l, eps_r, pair_e, out_ref,
    lraw, rraw, lt_own, rbuf, lt, relay, tbuf, tt, lm, ibuf, acc,
    sa, sb, xa1, xa2, yb1, yb2, sa3, sb3, ya3, ya4, xb3, xb4, a4, r4,
    own_sem, r_send, r_recv, t_send, t_recv, s1_send, s1_recv, h_send, h_recv, y_send, y_recv,
    k_send, k_recv, c_send, c_recv, x_send, x_recv, sum_send, sum_recv, z_send, z_recv,
    line_sem,
):
    f32, bf16 = jnp.float32, jnp.bfloat16
    row = lax.axis_index("row")
    col = lax.axis_index("col")
    x, zl = row % 4, row // 4
    y, zh, core = col // 4, (col // 2) % 2, col % 2
    z = zh * 8 + zl

    def dev(x_, y_, z_, core_):
        return {"row": (z_ % 8) * 4 + x_, "col": y_ * 4 + (z_ // 8) * 2 + core_}

    def remote(src, dst, send, recv, to):
        return pltpu.make_async_remote_copy(
            src_ref=src, dst_ref=dst, send_sem=send, recv_sem=recv, device_id=to, device_id_type=MESH
        )

    xp, xm, xo = (x + 1) % 4, (x + 3) % 4, (x + 2) % 4
    yp, ym, yo = (y + 1) % 4, (y + 3) % 4, (y + 2) % 4
    x_up, x_down = dev(xp, y, z, core), dev(xm, y, z, core)
    y_up, y_down = dev(x, yp, z, core), dev(x, ym, z, core)
    z_up, z_down = dev(x, y, (z + 1) % 16, core), dev(x, y, (z + 15) % 16, core)
    sibling = dev(x, y, z, 1 - core)

    barrier = pltpu.get_barrier_semaphore()
    partners = [dev((x + dx) % 4, y, z, (core + dc) % 2) for dx in (2, 1, 3, 0) for dc in range(2) if dx or dc]
    partners += [y_up, y_down, z_up, z_down]
    for partner in partners:
        pl.semaphore_signal(barrier, inc=1, device_id=partner, device_id_type=MESH)

    own = [
        pltpu.make_async_copy(right_ref, rraw, own_sem.at[0]),
        pltpu.make_async_copy(left_ref, lraw, own_sem.at[1]),
        pltpu.make_async_copy(amp_ref, tbuf.at[core, x], own_sem.at[2]),
    ]
    for copy in own:
        copy.start()

    own[1].wait()
    for half in range(2):
        lt_own[half] = lraw[:, half].reshape(256, 128).T
    own[2].wait()
    pl.semaphore_wait(barrier, len(partners))

    def heard(step):
        for way in range(2):
            pl.semaphore_wait(line_sem.at[step, way], 1)

    def tell(step):
        for way, to in enumerate((z_up, z_down)):
            pl.semaphore_signal(line_sem.at[step, way], inc=1, device_id=to, device_id_type=MESH)

    tell(0)

    s1 = []
    for h in range(2):
        for half in range(2):
            x_to = 2 * core + h
            here = (x_to == x) & (core == half)
            src = lt_own.at[half, pl.ds(64 * h, 64)]
            dst = lt.at[y, zh, x]
            away = remote(src, dst, s1_send.at[h, half], s1_recv.at[x], dev(x_to, y, z, half))
            local = pltpu.make_async_copy(src, dst, s1_recv.at[x])
            pl.when(jnp.logical_not(here))(away.start)
            pl.when(here)(local.start)
            s1.append((here, away))

    def right_copy(way, jc, s):
        origin = jnp.clip(zl - s, 0, 7) if way == 0 else jnp.clip(zl + s, 0, 7)
        block = rbuf.at[core, jc, origin]
        return remote(block, block, r_send.at[way, jc, s], r_recv.at[way, jc, s], z_up if way == 0 else z_down)

    def chip_copy(jc, origin):
        block = rbuf.at[core, jc, origin]
        return remote(block, block, c_send.at[jc, origin], c_recv.at[jc, origin], sibling)

    def slot(tau):
        for jc in range(4):
            s = tau - LAG * jc
            for way in range(2):
                reach = zl if way == 0 else 7 - zl
                if not isinstance(s, int) or 1 <= s <= 7:
                    came = right_copy(way, jc, jnp.clip(s - 1, 0, 6))
                    pl.when((s >= 1) & (s <= reach))(came.wait_recv)
                if not isinstance(s, int) or 0 <= s <= 6:
                    goes = right_copy(way, jc, jnp.clip(s, 0, 6))
                    pl.when((s >= 0) & (s <= reach) & (s <= 6) & (reach < 7))(goes.start)
                origin = jnp.clip(zl - s, 0, 7) if way == 0 else jnp.clip(zl + s, 0, 7)
                if not isinstance(s, int) or way <= s <= 7:
                    pl.when((s >= way) & (s <= reach))(chip_copy(jc, origin).start)

    t_a = [
        remote(tbuf.at[core, x], tbuf.at[core, x], t_send.at[0], t_recv.at[0], x_up),
        remote(tbuf.at[core, x], tbuf.at[core, x], t_send.at[1], t_recv.at[1], x_down),
    ]
    for copy in t_a:
        copy.start()
    share = [
        remote(tbuf.at[core, x_], tbuf.at[core, x_], k_send.at[i], k_recv.at[i], sibling)
        for i, x_ in enumerate((x, xm, xp, xo))
    ]
    share[0].start()

    r_id = lax.broadcasted_iota(jnp.int32, (256, 256), 0)
    c_id = lax.broadcasted_iota(jnp.int32, (256, 256), 1)
    swap = ((r_id // 16 == c_id % 16) & (r_id % 16 == c_id // 16)).astype(f32).astype(bf16)
    own[0].wait()
    for g in range(4):
        rows = []
        for q2 in range(8):
            low = rraw[0:16, 1024 * g + 128 * q2 : 1024 * g + 128 * q2 + 128]
            high = rraw[16:32, 1024 * g + 128 * q2 : 1024 * g + 128 * q2 + 128]
            rows.append(jnp.concatenate([low[:, :64], high[:, :64]], axis=1))
            rows.append(jnp.concatenate([low[:, 64:], high[:, 64:]], axis=1))
        turned = jnp.dot(swap, jnp.concatenate(rows, axis=0), preferred_element_type=f32)
        turned = turned.astype(bf16).reshape(4, 4, 16, 128)
        rbuf[core, :, zl, :, 16 * g : 16 * g + 16, :] = turned
    heard(0)
    tell(1)
    slot(0)

    for m in range(4):
        pltpu.make_async_copy(lt.at[0, 0, 0], lt.at[0, 0, 0], s1_recv.at[m]).wait()
    heard(1)
    tell(2)
    heard(2)
    tell(3)
    ahead = jnp.where(core == 0, (z + 4) % 16, (z + 12) % 16)
    behind = jnp.where(core == 0, (z + 12) % 16, (z + 4) % 16)
    hop1 = remote(lt.at[y, zh], relay, h_send.at[0], h_recv.at[0], dev(x, y, ahead, core))
    hop1.start()
    acc[...] = jnp.zeros_like(acc)
    slot(1)
    heard(3)
    tell(4)
    slot(2)
    heard(4)
    tell(5)
    hop1.wait_recv()
    hop2 = remote(relay, lt.at[y, behind // 8], h_send.at[1], h_recv.at[1], dev(x, y, ahead, core))
    hop2.start()
    heard(5)
    tell(6)
    slot(3)
    heard(6)
    for copy in t_a:
        copy.wait_recv()
    t_b = [
        remote(tbuf.at[core, xm, pl.ds(0, 8)], tbuf.at[core, xm, pl.ds(0, 8)], t_send.at[2], t_recv.at[2], x_up),
        remote(tbuf.at[core, xp, pl.ds(8, 8)], tbuf.at[core, xp, pl.ds(8, 8)], t_send.at[3], t_recv.at[3], x_down),
    ]
    for copy in t_b:
        copy.start()
    share[1].start()
    share[2].start()
    slot(4)
    hop2.wait_recv()
    y_a = [
        remote(lt.at[y], lt.at[y], y_send.at[0], y_recv.at[0], y_up),
        remote(lt.at[y], lt.at[y], y_send.at[1], y_recv.at[1], y_down),
    ]
    for copy in y_a:
        copy.start()
    for copy in t_b:
        copy.wait_recv()
    share[3].start()
    slot(5)
    for copy in y_a:
        copy.wait_recv()
    y_b = [
        remote(lt.at[ym, 0], lt.at[ym, 0], y_send.at[2], y_recv.at[2], y_up),
        remote(lt.at[yp, 1], lt.at[yp, 1], y_send.at[3], y_recv.at[3], y_down),
    ]
    for copy in y_b:
        copy.start()
    slot(6)
    for copy in share:
        copy.wait_recv()

    r_id = lax.broadcasted_iota(jnp.int32, (512, 128), 0)
    c_id = lax.broadcasted_iota(jnp.int32, (512, 128), 1)
    for side in range(2):
        for pair in range(2):
            for half in range(2):
                both = [tbuf[side, 2 * pair + i, :, 16 * half : 16 * half + 16, :].reshape(256, 256) for i in range(2)]
                turned = jnp.concatenate(both, axis=0).T
                for jc in range(4):
                    pick = (r_id // 256 == c_id // 64) & ((r_id // 16) % 16 == c_id % 16) & (r_id % 16 == 4 * jc + (c_id // 16) % 4)
                    value = jnp.dot(turned, pick.astype(f32).astype(bf16), preferred_element_type=f32)
                    at = 512 * side + 256 * half + 128 * pair
                    tt[jc, :, at : at + 128] = value.astype(bf16)

    for copy in y_b:
        copy.wait_recv()
    for xs in range(4):
        lm[xs] = lt[:, :, xs].reshape(512, 256).T
    slot(7)

    def integrals(jc):
        for step, side in enumerate((core, 1 - core)):
            if step == 1:
                for origin in range(8):
                    chip_copy(jc, origin).wait_recv()

            @pl.loop(0, 2)
            def _(n):
                right = jnp.concatenate([rbuf[side, jc, :, 2 * n + i].reshape(512, 128) for i in range(2)], axis=1)
                for xs in range(4):
                    value = jnp.dot(lm[xs], right, preferred_element_type=f32)
                    ibuf[2 * side + n, xs] = value.astype(bf16).reshape(16, 16, 256)

    def ladder(jc, k):
        rows = []
        for side in range(2):
            columns = []
            for ai in range(4):
                tiles = [
                    ibuf[2 * side + j // 2, xs, 4 * k + ai, :, 128 * (j % 2) : 128 * (j % 2) + 128]
                    for xs in range(4) for j in range(4)
                ]
                columns.append(jnp.concatenate(tiles, axis=0))
            rows.append(jnp.concatenate([column[:, :64] for column in columns], axis=1))
            rows.append(jnp.concatenate([column[:, 64:] for column in columns], axis=1))
        value = jnp.dot(tt[jc], jnp.concatenate(rows, axis=0), preferred_element_type=f32)
        return value[:, :128], value[:, 128:]

    @pl.loop(0, 3)
    def _(jc):
        integrals(jc)
        slot(8 + jc)

        @pl.loop(0, 2)
        def _(i):
            for k in (2 * i, 2 * i + 1):
                one, two = ladder(jc, k)
                acc[2 * k] += one
                acc[2 * k + 1] += two

    integrals(3)

    def first_copy(way, k):
        return remote(sa.at[xo, k, way], xa1.at[way, k], x_send.at[way, k], x_recv.at[way, k], (x_up, x_down)[way])

    def last_ladder(k):
        parts = ladder(3, k)
        for m in range(2):
            value = (acc[2 * k + m] + parts[m]).reshape(2, 4, 4, 8, 128)
            sa[:, k, m] = value[0].transpose(1, 0, 2, 3)
            sb[k, m] = value[1].transpose(1, 0, 2, 3)
        for way in range(2):
            first_copy(way, k).start()

    def sums(k, up_src, up_dst, down_src, down_dst, up, down):
        copies = [
            remote(up_src, up_dst, sum_send.at[k, 0], sum_recv.at[k, 0], up),
            remote(down_src, down_dst, sum_send.at[k, 1], sum_recv.at[k, 1], down),
        ]
        for copy in copies:
            copy.start()
        return copies

    last_ladder(yo)
    b_1 = sums(1, sb.at[yo, 0], yb1.at[0], sb.at[yo, 1], yb1.at[1], y_up, y_down)

    @pl.loop(1, 4)
    def _(k):
        last_ladder((yo + k) % 4)

    for way, x_ in enumerate((xp, xm)):
        for k in range(4):
            first_copy(way, k).wait_recv()
        sa[x_, :, way] += xa1[way]
    a_2 = sums(2, sa.at[xp], xa2.at[0], sa.at[xm], xa2.at[1], x_up, x_down)
    b_1[0].wait_recv()
    sb[yp, 0] += yb1[0]
    b_1[1].wait_recv()
    sb[ym, 1] += yb1[1]
    b_2 = sums(3, sb.at[yp], yb2.at[0], sb.at[ym], yb2.at[1], y_up, y_down)
    for copy in a_2:
        copy.wait_recv()
    sa3[...] = sa[x] + xa2[0] + xa2[1]
    a_3 = sums(4, sa3.at[yo, 0], ya3.at[0], sa3.at[yo, 1], ya3.at[1], y_up, y_down)
    for copy in b_2:
        copy.wait_recv()
    sb3[...] = (sb[y] + yb2[0] + yb2[1]).transpose(1, 0, 2, 3, 4)
    b_3 = sums(5, sb3.at[xo, 0], xb3.at[0], sb3.at[xo, 1], xb3.at[1], x_up, x_down)
    for copy in a_3:
        copy.wait_recv()
    sa3[yp, 0] += ya3[0]
    sa3[ym, 1] += ya3[1]
    a_4 = sums(6, sa3.at[yp], ya4.at[0], sa3.at[ym], ya4.at[1], y_up, y_down)
    for copy in b_3:
        copy.wait_recv()
    sb3[xp, 0] += xb3[0]
    sb3[xm, 1] += xb3[1]
    b_4 = sums(7, sb3.at[xp], xb4.at[0], sb3.at[xm], xb4.at[1], x_up, x_down)
    def z_copy(dz):
        to = (z + dz) % 16
        return remote(a4.at[to // 8, to % 8], r4.at[dz - 1], z_send.at[dz - 1], z_recv.at[dz - 1], dev(x, y, to, core))

    order = (8, 7, 9, 6, 10, 5, 11, 4, 12, 3, 13, 2, 14, 1, 15)
    for copy in a_4:
        copy.wait_recv()
    a4[:, 0:4] = sa3[y] + ya4[0] + ya4[1]
    for dz in order:
        pl.when((z + dz) % 8 < 4)(z_copy(dz).start)
    for copy in b_4:
        copy.wait_recv()
    a4[:, 4:8] = sb3[x] + xb4[0] + xb4[1]
    for dz in order:
        pl.when((z + dz) % 8 >= 4)(z_copy(dz).start)
    total = a4[zh, zl]
    for dz in order[::-1]:
        z_copy(dz).wait_recv()
        total = total + r4[dz - 1]
    pair = lax.broadcasted_iota(jnp.int32, (8, 64), 0)
    energy = jnp.full((8, 64), pair_e[0], f32)
    for i in range(1, 8):
        energy = jnp.where(pair == i, pair_e[i], energy)
    for i in range(2):
        out_ref[:, i, :] = total[:, 64 * i : 64 * i + 64] / (eps_l[i] + eps_r[...] - energy)

    for here, away in s1:
        pl.when(jnp.logical_not(here))(away.wait_send)

    @pl.loop(0, 7)
    def _(s):
        for jc in range(4):
            pl.when((s <= zl) & (zl < 7))(right_copy(0, jc, s).wait_send)
            pl.when((s <= 7 - zl) & (zl > 0))(right_copy(1, jc, s).wait_send)

    for jc in range(4):
        for origin in range(8):
            chip_copy(jc, origin).wait_send()

    for copy in [hop1, hop2] + t_a + t_b + y_a + y_b + share + b_1 + a_2 + b_2 + a_3 + b_3 + a_4 + b_4:
        copy.wait_send()
    for way in range(2):
        for k in range(4):
            first_copy(way, k).wait_send()
    for dz in order:
        z_copy(dz).wait_send()


def per_device(left_factors, right_factors, amplitudes, eps_left, eps_right, pair_energy):
    bf16, f32 = jnp.bfloat16, jnp.float32
    dma = pltpu.SemaphoreType.DMA
    return pl.pallas_call(
        fused,
        out_shape=jax.ShapeDtypeStruct((8, 2, 64), f32),
        in_specs=[pl.BlockSpec(memory_space=pl.ANY)] * 3
        + [pl.BlockSpec(memory_space=space) for space in (pltpu.SMEM, pltpu.VMEM, pltpu.SMEM)],
        out_specs=pl.BlockSpec(memory_space=pltpu.VMEM),
        scratch_shapes=[
            pltpu.VMEM((8, 2, 2, 16, 128), bf16),
            pltpu.VMEM((32, 4096), bf16),
            pltpu.VMEM((2, 128, 256), bf16),
            pltpu.VMEM((2, 4, 8, 4, 64, 128), bf16),
            pltpu.VMEM((4, 2, 4, 64, 256), bf16),
            pltpu.VMEM((4, 64, 256), bf16),
            pltpu.VMEM((2, 4, 16, 32, 256), bf16),
            pltpu.VMEM((4, 256, 1024), bf16),
            pltpu.VMEM((4, 256, 512), bf16),
            pltpu.VMEM((4, 4, 16, 16, 256), bf16),
            pltpu.VMEM((8, 256, 128), f32),
            pltpu.VMEM((4, 4, 2, 4, 8, 128), f32),
            pltpu.VMEM((4, 2, 4, 4, 8, 128), f32),
            pltpu.VMEM((2, 4, 4, 8, 128), f32),
            pltpu.VMEM((2, 4, 2, 4, 8, 128), f32),
            pltpu.VMEM((2, 4, 4, 8, 128), f32),
            pltpu.VMEM((2, 2, 4, 4, 8, 128), f32),
            pltpu.VMEM((4, 2, 4, 8, 128), f32),
            pltpu.VMEM((4, 2, 4, 8, 128), f32),
            pltpu.VMEM((2, 4, 8, 128), f32),
            pltpu.VMEM((2, 2, 4, 8, 128), f32),
            pltpu.VMEM((2, 4, 8, 128), f32),
            pltpu.VMEM((2, 2, 4, 8, 128), f32),
            pltpu.VMEM((2, 8, 8, 128), f32),
            pltpu.VMEM((15, 8, 128), f32),
            dma((3,)),
            dma((2, 4, 7)), dma((2, 4, 7)),
            dma((4,)), dma((4,)),
            dma((2, 2)), dma((4,)),
            dma((2,)), dma((2,)),
            dma((4,)), dma((4,)),
            dma((4,)), dma((4,)),
            dma((4, 8)), dma((4, 8)),
            dma((2, 4)), dma((2, 4)),
            dma((8, 2)), dma((8, 2)),
            dma((15,)), dma((15,)),
            pltpu.SemaphoreType.REGULAR((7, 2)),
        ],
        compiler_params=pltpu.CompilerParams(
            collective_id=0, has_side_effects=True, vmem_limit_bytes=60 * 1024 * 1024
        ),
    )(
        left_factors.reshape(8, 2, 2, 16, 128), right_factors, amplitudes,
        eps_left, eps_right.reshape(1, 64), pair_energy,
    )


def solution(mesh):
    in_specs = (
        P(None, "row", "col"),
        P("col", "row"),
        P("row", "col", None),
        P("col"),
        P(),
        P("row"),
    )
    out_specs = P("row", "col", None)
    return jax.shard_map(
        per_device, mesh=mesh, in_specs=in_specs, out_specs=out_specs, check_vma=False
    )
```

```python
import jax
import jax.numpy as jnp
from jax import lax
from jax.experimental import pallas as pl
from jax.experimental.pallas import tpu as pltpu
from jax.sharding import PartitionSpec as P

MESH = pl.DeviceIdType.MESH
LAG = 1


def fused(
    left_ref, right_ref, amp_ref, eps_l, eps_r, pair_e, out_ref,
    lraw, rraw, lt_own, rbuf, lt, relay, tbuf, tt, lm, ibuf, acc,
    sa, sb, xa1, xa2, yb1, yb2, sa3, sb3, ya3, ya4, xb3, xb4, a4, r4,
    own_sem, r_send, r_recv, t_send, t_recv, s1_send, s1_recv, h_send, h_recv, y_send, y_recv,
    k_send, k_recv, c_send, c_recv, x_send, x_recv, sum_send, sum_recv, z_send, z_recv,
    line_sem,
):
    f32, bf16 = jnp.float32, jnp.bfloat16
    row = lax.axis_index("row")
    col = lax.axis_index("col")
    x, zl = row % 4, row // 4
    y, zh, core = col // 4, (col // 2) % 2, col % 2
    z = zh * 8 + zl

    def dev(x_, y_, z_, core_):
        return {"row": (z_ % 8) * 4 + x_, "col": y_ * 4 + (z_ // 8) * 2 + core_}

    def remote(src, dst, send, recv, to):
        return pltpu.make_async_remote_copy(
            src_ref=src, dst_ref=dst, send_sem=send, recv_sem=recv, device_id=to, device_id_type=MESH
        )

    xp, xm, xo = (x + 1) % 4, (x + 3) % 4, (x + 2) % 4
    yp, ym, yo = (y + 1) % 4, (y + 3) % 4, (y + 2) % 4
    x_up, x_down = dev(xp, y, z, core), dev(xm, y, z, core)
    y_up, y_down = dev(x, yp, z, core), dev(x, ym, z, core)
    z_up, z_down = dev(x, y, (z + 1) % 16, core), dev(x, y, (z + 15) % 16, core)
    sibling = dev(x, y, z, 1 - core)

    barrier = pltpu.get_barrier_semaphore()
    partners = [dev((x + dx) % 4, y, z, (core + dc) % 2) for dx in (2, 1, 3, 0) for dc in range(2) if dx or dc]
    partners += [y_up, y_down, z_up, z_down]
    for partner in partners:
        pl.semaphore_signal(barrier, inc=1, device_id=partner, device_id_type=MESH)

    own = [
        pltpu.make_async_copy(right_ref, rraw, own_sem.at[0]),
        pltpu.make_async_copy(left_ref, lraw, own_sem.at[1]),
        pltpu.make_async_copy(amp_ref, tbuf.at[core, x], own_sem.at[2]),
    ]
    for copy in own:
        copy.start()

    own[1].wait()
    for half in range(2):
        lt_own[half] = lraw[:, half].reshape(256, 128).T
    own[2].wait()
    pl.semaphore_wait(barrier, len(partners))

    def heard(step):
        for way in range(2):
            pl.semaphore_wait(line_sem.at[step, way], 1)

    def tell(step):
        for way, to in enumerate((z_up, z_down)):
            pl.semaphore_signal(line_sem.at[step, way], inc=1, device_id=to, device_id_type=MESH)

    tell(0)

    s1 = []
    for h in range(2):
        for half in range(2):
            x_to = 2 * core + h
            here = (x_to == x) & (core == half)
            src = lt_own.at[half, pl.ds(64 * h, 64)]
            dst = lt.at[y, zh, x]
            away = remote(src, dst, s1_send.at[h, half], s1_recv.at[x], dev(x_to, y, z, half))
            local = pltpu.make_async_copy(src, dst, s1_recv.at[x])
            pl.when(jnp.logical_not(here))(away.start)
            pl.when(here)(local.start)
            s1.append((here, away))

    def right_copy(way, jc, s):
        origin = jnp.clip(zl - s, 0, 7) if way == 0 else jnp.clip(zl + s, 0, 7)
        block = rbuf.at[core, jc, origin]
        return remote(block, block, r_send.at[way, jc, s], r_recv.at[way, jc, s], z_up if way == 0 else z_down)

    def chip_copy(jc, origin):
        block = rbuf.at[core, jc, origin]
        return remote(block, block, c_send.at[jc, origin], c_recv.at[jc, origin], sibling)

    def slot(tau):
        for jc in range(4):
            s = tau - LAG * jc
            for way in range(2):
                reach = zl if way == 0 else 7 - zl
                if not isinstance(s, int) or 1 <= s <= 7:
                    came = right_copy(way, jc, jnp.clip(s - 1, 0, 6))
                    pl.when((s >= 1) & (s <= reach))(came.wait_recv)
                if not isinstance(s, int) or 0 <= s <= 6:
                    goes = right_copy(way, jc, jnp.clip(s, 0, 6))
                    pl.when((s >= 0) & (s <= reach) & (s <= 6) & (reach < 7))(goes.start)
                origin = jnp.clip(zl - s, 0, 7) if way == 0 else jnp.clip(zl + s, 0, 7)
                if not isinstance(s, int) or way <= s <= 7:
                    pl.when((s >= way) & (s <= reach))(chip_copy(jc, origin).start)

    t_a = [
        remote(tbuf.at[core, x], tbuf.at[core, x], t_send.at[0], t_recv.at[0], x_up),
        remote(tbuf.at[core, x], tbuf.at[core, x], t_send.at[1], t_recv.at[1], x_down),
    ]
    for copy in t_a:
        copy.start()
    share = [
        remote(tbuf.at[core, x_], tbuf.at[core, x_], k_send.at[i], k_recv.at[i], sibling)
        for i, x_ in enumerate((x, xm, xp, xo))
    ]
    share[0].start()

    r_id = lax.broadcasted_iota(jnp.int32, (256, 256), 0)
    c_id = lax.broadcasted_iota(jnp.int32, (256, 256), 1)
    swap = ((r_id // 16 == c_id % 16) & (r_id % 16 == c_id // 16)).astype(f32).astype(bf16)
    own[0].wait()
    for g in range(4):
        rows = []
        for q2 in range(8):
            low = rraw[0:16, 1024 * g + 128 * q2 : 1024 * g + 128 * q2 + 128]
            high = rraw[16:32, 1024 * g + 128 * q2 : 1024 * g + 128 * q2 + 128]
            rows.append(jnp.concatenate([low[:, :64], high[:, :64]], axis=1))
            rows.append(jnp.concatenate([low[:, 64:], high[:, 64:]], axis=1))
        turned = jnp.dot(swap, jnp.concatenate(rows, axis=0), preferred_element_type=f32)
        turned = turned.astype(bf16).reshape(4, 4, 16, 128)
        rbuf[core, :, zl, :, 16 * g : 16 * g + 16, :] = turned
    heard(0)
    tell(1)
    slot(0)

    for m in range(4):
        pltpu.make_async_copy(lt.at[0, 0, 0], lt.at[0, 0, 0], s1_recv.at[m]).wait()
    heard(1)
    tell(2)
    heard(2)
    tell(3)
    ahead = jnp.where(core == 0, (z + 4) % 16, (z + 12) % 16)
    behind = jnp.where(core == 0, (z + 12) % 16, (z + 4) % 16)
    hop1 = remote(lt.at[y, zh], relay, h_send.at[0], h_recv.at[0], dev(x, y, ahead, core))
    hop1.start()
    y_a = [
        remote(lt.at[y, zh], lt.at[y, zh], y_send.at[0], y_recv.at[0], y_up),
        remote(lt.at[y, zh], lt.at[y, zh], y_send.at[1], y_recv.at[1], y_down),
    ]
    for copy in y_a:
        copy.start()
    acc[...] = jnp.zeros_like(acc)
    slot(1)
    heard(3)
    tell(4)
    slot(2)
    heard(4)
    tell(5)
    hop1.wait_recv()
    hop2 = remote(relay, lt.at[y, behind // 8], h_send.at[1], h_recv.at[1], dev(x, y, ahead, core))
    hop2.start()
    heard(5)
    tell(6)
    slot(3)
    heard(6)
    for copy in t_a:
        copy.wait_recv()
    t_b = [
        remote(tbuf.at[core, xm, pl.ds(0, 8)], tbuf.at[core, xm, pl.ds(0, 8)], t_send.at[2], t_recv.at[2], x_up),
        remote(tbuf.at[core, xp, pl.ds(8, 8)], tbuf.at[core, xp, pl.ds(8, 8)], t_send.at[3], t_recv.at[3], x_down),
    ]
    for copy in t_b:
        copy.start()
    share[1].start()
    share[2].start()
    slot(4)
    hop2.wait_recv()
    y_a += [
        remote(lt.at[y, 1 - zh], lt.at[y, 1 - zh], y_send.at[4], y_recv.at[4], y_up),
        remote(lt.at[y, 1 - zh], lt.at[y, 1 - zh], y_send.at[5], y_recv.at[5], y_down),
    ]
    for copy in y_a[2:]:
        copy.start()
    for copy in t_b:
        copy.wait_recv()
    share[3].start()
    slot(5)
    for copy in y_a:
        copy.wait_recv()
    y_b = [
        remote(lt.at[ym, 0], lt.at[ym, 0], y_send.at[2], y_recv.at[2], y_up),
        remote(lt.at[yp, 1], lt.at[yp, 1], y_send.at[3], y_recv.at[3], y_down),
    ]
    for copy in y_b:
        copy.start()
    slot(6)
    for copy in share:
        copy.wait_recv()

    r_id = lax.broadcasted_iota(jnp.int32, (512, 128), 0)
    c_id = lax.broadcasted_iota(jnp.int32, (512, 128), 1)
    for side in range(2):
        for pair in range(2):
            for half in range(2):
                both = [tbuf[side, 2 * pair + i, :, 16 * half : 16 * half + 16, :].reshape(256, 256) for i in range(2)]
                turned = jnp.concatenate(both, axis=0).T
                for jc in range(4):
                    pick = (r_id // 256 == c_id // 64) & ((r_id // 16) % 16 == c_id % 16) & (r_id % 16 == 4 * jc + (c_id // 16) % 4)
                    value = jnp.dot(turned, pick.astype(f32).astype(bf16), preferred_element_type=f32)
                    at = 512 * side + 256 * half + 128 * pair
                    tt[jc, :, at : at + 128] = value.astype(bf16)

    for copy in y_b:
        copy.wait_recv()
    for xs in range(4):
        lm[xs] = lt[:, :, xs].reshape(512, 256).T
    slot(7)

    def integrals(jc):
        for step, side in enumerate((core, 1 - core)):
            if step == 1:
                for origin in range(8):
                    chip_copy(jc, origin).wait_recv()

            @pl.loop(0, 2)
            def _(n):
                right = jnp.concatenate([rbuf[side, jc, :, 2 * n + i].reshape(512, 128) for i in range(2)], axis=1)
                for xs in range(4):
                    value = jnp.dot(lm[xs], right, preferred_element_type=f32)
                    ibuf[2 * side + n, xs] = value.astype(bf16).reshape(16, 16, 256)

    def ladder(jc, k):
        rows = []
        for side in range(2):
            columns = []
            for ai in range(4):
                tiles = [
                    ibuf[2 * side + j // 2, xs, 4 * k + ai, :, 128 * (j % 2) : 128 * (j % 2) + 128]
                    for xs in range(4) for j in range(4)
                ]
                columns.append(jnp.concatenate(tiles, axis=0))
            rows.append(jnp.concatenate([column[:, :64] for column in columns], axis=1))
            rows.append(jnp.concatenate([column[:, 64:] for column in columns], axis=1))
        value = jnp.dot(tt[jc], jnp.concatenate(rows, axis=0), preferred_element_type=f32)
        return value[:, :128], value[:, 128:]

    @pl.loop(0, 3)
    def _(jc):
        integrals(jc)
        slot(8 + jc)

        @pl.loop(0, 2)
        def _(i):
            for k in (2 * i, 2 * i + 1):
                one, two = ladder(jc, k)
                acc[2 * k] += one
                acc[2 * k + 1] += two

    integrals(3)

    def first_copy(way, k):
        return remote(sa.at[xo, k, way], xa1.at[way, k], x_send.at[way, k], x_recv.at[way, k], (x_up, x_down)[way])

    def last_ladder(k):
        parts = ladder(3, k)
        for m in range(2):
            value = (acc[2 * k + m] + parts[m]).reshape(2, 4, 4, 8, 128)
            sa[:, k, m] = value[0].transpose(1, 0, 2, 3)
            sb[k, m] = value[1].transpose(1, 0, 2, 3)
        for way in range(2):
            first_copy(way, k).start()

    def sums(k, up_src, up_dst, down_src, down_dst, up, down):
        copies = [
            remote(up_src, up_dst, sum_send.at[k, 0], sum_recv.at[k, 0], up),
            remote(down_src, down_dst, sum_send.at[k, 1], sum_recv.at[k, 1], down),
        ]
        for copy in copies:
            copy.start()
        return copies

    last_ladder(yo)
    b_1 = sums(1, sb.at[yo, 0], yb1.at[0], sb.at[yo, 1], yb1.at[1], y_up, y_down)

    @pl.loop(1, 4)
    def _(k):
        last_ladder((yo + k) % 4)

    for way, x_ in enumerate((xp, xm)):
        for k in range(4):
            first_copy(way, k).wait_recv()
        sa[x_, :, way] += xa1[way]
    a_2 = sums(2, sa.at[xp], xa2.at[0], sa.at[xm], xa2.at[1], x_up, x_down)
    b_1[0].wait_recv()
    sb[yp, 0] += yb1[0]
    b_1[1].wait_recv()
    sb[ym, 1] += yb1[1]
    b_2 = sums(3, sb.at[yp], yb2.at[0], sb.at[ym], yb2.at[1], y_up, y_down)
    for copy in a_2:
        copy.wait_recv()
    sa3[...] = sa[x] + xa2[0] + xa2[1]
    a_3 = sums(4, sa3.at[yo, 0], ya3.at[0], sa3.at[yo, 1], ya3.at[1], y_up, y_down)
    for copy in b_2:
        copy.wait_recv()
    sb3[...] = (sb[y] + yb2[0] + yb2[1]).transpose(1, 0, 2, 3, 4)
    b_3 = sums(5, sb3.at[xo, 0], xb3.at[0], sb3.at[xo, 1], xb3.at[1], x_up, x_down)
    for copy in a_3:
        copy.wait_recv()
    sa3[yp, 0] += ya3[0]
    sa3[ym, 1] += ya3[1]
    a_4 = sums(6, sa3.at[yp], ya4.at[0], sa3.at[ym], ya4.at[1], y_up, y_down)
    for copy in b_3:
        copy.wait_recv()
    sb3[xp, 0] += xb3[0]
    sb3[xm, 1] += xb3[1]
    b_4 = sums(7, sb3.at[xp], xb4.at[0], sb3.at[xm], xb4.at[1], x_up, x_down)
    def z_copy(dz):
        to = (z + dz) % 16
        return remote(a4.at[to // 8, to % 8], r4.at[dz - 1], z_send.at[dz - 1], z_recv.at[dz - 1], dev(x, y, to, core))

    order = (8, 7, 9, 6, 10, 5, 11, 4, 12, 3, 13, 2, 14, 1, 15)
    for copy in a_4:
        copy.wait_recv()
    a4[:, 0:4] = sa3[y] + ya4[0] + ya4[1]
    for dz in order:
        pl.when((z + dz) % 8 < 4)(z_copy(dz).start)
    for copy in b_4:
        copy.wait_recv()
    a4[:, 4:8] = sb3[x] + xb4[0] + xb4[1]
    for dz in order:
        pl.when((z + dz) % 8 >= 4)(z_copy(dz).start)
    total = a4[zh, zl]
    for dz in order[::-1]:
        z_copy(dz).wait_recv()
        total = total + r4[dz - 1]
    pair = lax.broadcasted_iota(jnp.int32, (8, 64), 0)
    energy = jnp.full((8, 64), pair_e[0], f32)
    for i in range(1, 8):
        energy = jnp.where(pair == i, pair_e[i], energy)
    for i in range(2):
        out_ref[:, i, :] = total[:, 64 * i : 64 * i + 64] / (eps_l[i] + eps_r[...] - energy)

    for here, away in s1:
        pl.when(jnp.logical_not(here))(away.wait_send)

    @pl.loop(0, 7)
    def _(s):
        for jc in range(4):
            pl.when((s <= zl) & (zl < 7))(right_copy(0, jc, s).wait_send)
            pl.when((s <= 7 - zl) & (zl > 0))(right_copy(1, jc, s).wait_send)

    for jc in range(4):
        for origin in range(8):
            chip_copy(jc, origin).wait_send()

    for copy in [hop1, hop2] + t_a + t_b + y_a + y_b + share + b_1 + a_2 + b_2 + a_3 + b_3 + a_4 + b_4:
        copy.wait_send()
    for way in range(2):
        for k in range(4):
            first_copy(way, k).wait_send()
    for dz in order:
        z_copy(dz).wait_send()


def per_device(left_factors, right_factors, amplitudes, eps_left, eps_right, pair_energy):
    bf16, f32 = jnp.bfloat16, jnp.float32
    dma = pltpu.SemaphoreType.DMA
    return pl.pallas_call(
        fused,
        out_shape=jax.ShapeDtypeStruct((8, 2, 64), f32),
        in_specs=[pl.BlockSpec(memory_space=pl.ANY)] * 3
        + [pl.BlockSpec(memory_space=space) for space in (pltpu.SMEM, pltpu.VMEM, pltpu.SMEM)],
        out_specs=pl.BlockSpec(memory_space=pltpu.VMEM),
        scratch_shapes=[
            pltpu.VMEM((8, 2, 2, 16, 128), bf16),
            pltpu.VMEM((32, 4096), bf16),
            pltpu.VMEM((2, 128, 256), bf16),
            pltpu.VMEM((2, 4, 8, 4, 64, 128), bf16),
            pltpu.VMEM((4, 2, 4, 64, 256), bf16),
            pltpu.VMEM((4, 64, 256), bf16),
            pltpu.VMEM((2, 4, 16, 32, 256), bf16),
            pltpu.VMEM((4, 256, 1024), bf16),
            pltpu.VMEM((4, 256, 512), bf16),
            pltpu.VMEM((4, 4, 16, 16, 256), bf16),
            pltpu.VMEM((8, 256, 128), f32),
            pltpu.VMEM((4, 4, 2, 4, 8, 128), f32),
            pltpu.VMEM((4, 2, 4, 4, 8, 128), f32),
            pltpu.VMEM((2, 4, 4, 8, 128), f32),
            pltpu.VMEM((2, 4, 2, 4, 8, 128), f32),
            pltpu.VMEM((2, 4, 4, 8, 128), f32),
            pltpu.VMEM((2, 2, 4, 4, 8, 128), f32),
            pltpu.VMEM((4, 2, 4, 8, 128), f32),
            pltpu.VMEM((4, 2, 4, 8, 128), f32),
            pltpu.VMEM((2, 4, 8, 128), f32),
            pltpu.VMEM((2, 2, 4, 8, 128), f32),
            pltpu.VMEM((2, 4, 8, 128), f32),
            pltpu.VMEM((2, 2, 4, 8, 128), f32),
            pltpu.VMEM((2, 8, 8, 128), f32),
            pltpu.VMEM((15, 8, 128), f32),
            dma((3,)),
            dma((2, 4, 7)), dma((2, 4, 7)),
            dma((6,)), dma((6,)),
            dma((2, 2)), dma((4,)),
            dma((2,)), dma((2,)),
            dma((6,)), dma((6,)),
            dma((6,)), dma((6,)),
            dma((4, 8)), dma((4, 8)),
            dma((2, 4)), dma((2, 4)),
            dma((8, 2)), dma((8, 2)),
            dma((15,)), dma((15,)),
            pltpu.SemaphoreType.REGULAR((7, 2)),
        ],
        compiler_params=pltpu.CompilerParams(
            collective_id=0, has_side_effects=True, vmem_limit_bytes=60 * 1024 * 1024
        ),
    )(
        left_factors.reshape(8, 2, 2, 16, 128), right_factors, amplitudes,
        eps_left, eps_right.reshape(1, 64), pair_energy,
    )


def solution(mesh):
    in_specs = (
        P(None, "row", "col"),
        P("col", "row"),
        P("row", "col", None),
        P("col"),
        P(),
        P("row"),
    )
    out_specs = P("row", "col", None)
    return jax.shard_map(
        per_device, mesh=mesh, in_specs=in_specs, out_specs=out_specs, check_vma=False
    )
```
